32 devices in a mesh: grp: 4 (over y, core), sp: 8 (over z, x).
Axes of the slice: x: 2, y: 2, z: 4, core: 2. Of those that a mesh axis runs over, the one named last changes fastest.
Arguments:
- flame_state: float32 [54, 16, 512], P(None, 'sp', 'grp'), may hold values from -1 to 2, as said below
- tangents: float32 [12, 54, 16, 512], P('grp', None, 'sp'), may hold values from -6 to 6
- direction_index: int32 [12], P('grp'), may hold values from 0 to 324
- reactant_table: int32 [325, 53], replicated, may hold values from 0 to 2, as said below
- product_table: int32 [325, 53], replicated, may hold values from 0 to 2, as said below
- natural_log_frequency: float32 [325], replicated, may hold values from -3 to -1
- arrhenius_energy: float32 [325], replicated, may hold values from 0.5 to 3
- diffusivity: float32 [54], replicated, may hold values from 0.03 to 0.25
- enthalpy: float32 [53], replicated, may hold values from -0.5 to 0.5
Outputs:
- new_state: float32 [54, 16, 512], P(None, 'sp', 'grp')
- new_tangents: float32 [12, 54, 16, 512], P('grp', None, 'sp')
The draws below stay inside these ranges and needn't reach their ends.
Inputs may be any that keep to these rules, and one draw needn't show every extreme that they name: `flame_state`: rows 0 to 52 are log concentrations in [-1, 0.5]; the last row is temperature in [1, 2]. `reactant_table`: each reaction has one or two reactant units; a species may count twice. `product_table`: each reaction has one or two product units; a species may count twice.
All inputs are finite; a program needn't handle non-finite values.
Results may differ from the reference program's by a relative error of at most 0.0003.
Values sent between devices are 32-bit elements; how exact they have to be, the bound alone decides.
A program may use at most 128 MiB of HBM per device.

```python
import math
import jax
import jax.numpy as jnp
from jax import lax

SPECIES = 53
REACTIONS = 325
FIELDS = 54
GRID_POINTS_TWO = 16
GRID_POINTS_THREE = 32
CELLS = 512
GRID_POINTS_ONE = 16
DIRECTIONS = 12


def draw_flame_state(key, part):
    component_seed_handle, thermal_seed_handle = jax.random.split(key)
    exponent_numbers = jax.random.uniform(component_seed_handle, (SPECIES, GRID_POINTS_ONE, GRID_POINTS_TWO * GRID_POINTS_THREE), jnp.float32, -1.0, 0.5)
    mixture_heat_level = jax.random.uniform(thermal_seed_handle, (1, GRID_POINTS_ONE, GRID_POINTS_TWO * GRID_POINTS_THREE), jnp.float32, 1.0, 2.0)
    return jnp.concatenate([exponent_numbers, mixture_heat_level], 0)


def stoich(key):
    leading_key, partner_key, doubled_key = jax.random.split(key, 3)
    leading = jax.random.randint(leading_key, (REACTIONS,), 0, SPECIES)
    partner = jax.random.randint(partner_key, (REACTIONS,), 0, SPECIES)
    doubled = jax.random.randint(doubled_key, (REACTIONS,), 0, 2)
    reaction_ids = jnp.arange(REACTIONS, dtype=jnp.int32)
    partner = jnp.where(reaction_ids == 0, leading, partner)
    doubled = jnp.where(reaction_ids == 0, 1, doubled)
    species_ids = jnp.arange(SPECIES, dtype=jnp.int32)
    single = (leading[:, None] == species_ids[None, :]).astype(jnp.int32)
    second_unit = (partner[:, None] == species_ids[None, :]).astype(jnp.int32)
    return single + doubled[:, None] * second_unit


def draw_reactant_table(key, part):
    return stoich(jax.random.fold_in(key, 11))


def draw_product_table(key, part):
    return stoich(jax.random.fold_in(key, 23))


def touch_ends(drawn, stream_key, low, high):
    longest = drawn.shape.index(max(drawn.shape))
    spots = []
    for shift in (0, 1):
        where = [jax.random.randint(jax.random.fold_in(stream_key, axis), (), 0, length) for axis, length in enumerate(drawn.shape)]
        where[longest] = (where[longest] + shift) % drawn.shape[longest]
        spots.append(tuple(where))
    return drawn.at[spots[0]].set(low).at[spots[1]].set(high)


def levels(rng, dims, cuts, low, largest):
    level = 1.0
    for dim, shards_of in cuts:
        steps = jax.random.uniform(jax.random.fold_in(jax.random.fold_in(rng, 6), dim), (shards_of,), jnp.float32, low / len(cuts), largest / len(cuts))
        level = level * jnp.repeat(jnp.exp(steps), dims[dim] // shards_of).reshape((-1,) + (1,) * (len(dims) - 1 - dim))
    return level


def bell_draw(rng, extent, width, bound, cuts=(), kind=jnp.bfloat16):
    values = jax.random.normal(rng, extent, jnp.float32) * width
    if len(cuts) > 0:
        values = levels(rng, extent, cuts, -0.22, 0.18) * values
    return jnp.clip(values, min=-bound, max=bound).astype(kind)


def setup_inputs(seed: int = 0) -> dict:
    seeds = jax.random.split(jax.random.key(seed), 10)
    flame_state = draw_flame_state(jax.random.fold_in(seeds[9], 71), 0)
    tangents = bell_draw(seeds[1], (DIRECTIONS, FIELDS, GRID_POINTS_ONE, CELLS), 1.0, 6.0, ((0, 4), (2, 8)), jnp.float32)
    direction_index = touch_ends(jax.random.randint(seeds[2], (DIRECTIONS,), 0, REACTIONS), jax.random.fold_in(seeds[2], 1), 0, REACTIONS - 1).astype(jnp.int32)
    reactant_table = draw_reactant_table(jax.random.fold_in(seeds[9], 71), 0)
    product_table = draw_product_table(jax.random.fold_in(seeds[9], 71), 0)
    natural_log_frequency = jnp.clip(jax.random.uniform(seeds[5], (REACTIONS,), jnp.float32, -3.0, -1.0), -3.0, -1.0)
    arrhenius_energy = jnp.clip(jnp.exp(jax.random.uniform(seeds[6], (REACTIONS,), jnp.float32, math.log(0.5), math.log(3.0))), 0.5, 3.0)
    diffusivity = jnp.clip(jnp.exp(jax.random.uniform(seeds[7], (FIELDS,), jnp.float32, math.log(0.03), math.log(0.25))), 0.03, 0.25)
    enthalpy = bell_draw(seeds[8], (SPECIES,), 0.1, 0.5, (), jnp.float32)
    return {"flame_state": flame_state, "tangents": tangents, "direction_index": direction_index, "reactant_table": reactant_table, "product_table": product_table, "natural_log_frequency": natural_log_frequency, "arrhenius_energy": arrhenius_energy, "diffusivity": diffusivity, "enthalpy": enthalpy}


time_step = 0.2
maximum_magnitude = lax.Precision.HIGHEST


def blockwise(kernel, arrays, block_cells):
    blocks = arrays[0].shape[-1] // block_cells

    def advance(block_id, results):
        offset = (block_id * block_cells).astype(jnp.int32)
        pieces = [lax.dynamic_slice_in_dim(operand_array, offset, block_cells, operand_array.ndim - 1) for operand_array in arrays]
        stored_numbers = kernel(*pieces)
        return tuple(lax.dynamic_update_slice_in_dim(result, value, offset, result.ndim - 1) for result, value in zip(results, stored_numbers))

    return lax.fori_loop(0, blocks, advance, tuple(jnp.zeros_like(operand_array) for operand_array in arrays))


def progress(stored_numbers, tables):
    consumed_multipliers, nu_net, natural_log_frequency, arrhenius_energy, enthalpy = tables
    exponent_numbers = stored_numbers[:-1]
    mixture_heat_level = stored_numbers[-1]
    exponent_speed = natural_log_frequency[:, None] - arrhenius_energy[:, None] / mixture_heat_level[None, :] + jnp.dot(consumed_multipliers, exponent_numbers, precision=maximum_magnitude)
    reaction_rates = jnp.exp(exponent_speed)
    production = jnp.dot(nu_net.T, reaction_rates, precision=maximum_magnitude)
    return reaction_rates, production


def nominal_chem(stored_numbers, tables):
    reaction_rates, production = progress(stored_numbers, tables)
    heat_term = -jnp.dot(tables[4], production, precision=maximum_magnitude)
    return (jnp.concatenate([production * jnp.exp(-stored_numbers[:-1]), heat_term[None, :]], 0),)


def joint_chem(stored_numbers, derivative_direction, selection_filter, tables):
    consumed_multipliers, nu_net, natural_log_frequency, arrhenius_energy, enthalpy = tables
    reaction_rates, production = progress(stored_numbers, tables)
    mixture_heat_level = stored_numbers[-1]
    inverse = jnp.exp(-stored_numbers[:-1])
    tangent_logs = derivative_direction[:, :-1]
    derivative_thermal_field = derivative_direction[:, -1]
    exponent_shift = selection_filter[:, :, None] + (arrhenius_energy[None, :, None] / (mixture_heat_level * mixture_heat_level)[None, None, :]) * derivative_thermal_field[:, None, :]
    exponent_shift = exponent_shift + jnp.einsum("rs,dsb->drb", consumed_multipliers, tangent_logs, precision=maximum_magnitude)
    production_change = jnp.einsum("rs,drb->dsb", nu_net, reaction_rates[None] * exponent_shift, precision=maximum_magnitude)
    heat_change = -jnp.einsum("s,dsb->db", enthalpy, production_change, precision=maximum_magnitude)
    heat_term = -jnp.dot(enthalpy, production, precision=maximum_magnitude)
    nominal = jnp.concatenate([production * inverse, heat_term[None, :]], 0)
    tangent_change = jnp.concatenate([(production_change - production[None] * tangent_logs) * inverse[None], heat_change[:, None, :]], 1)
    return nominal, tangent_change


def laplace(field_values, leading):
    summed = -6.0 * field_values
    for dimension in range(leading, leading + 3):
        summed = summed + jnp.roll(field_values, 1, dimension) + jnp.roll(field_values, -1, dimension)
    return summed


def reference(flame_state, tangents, direction_index, reactant_table, product_table, natural_log_frequency, arrhenius_energy, diffusivity, enthalpy):
    tables = (reactant_table.astype(jnp.float32), (product_table - reactant_table).astype(jnp.float32), natural_log_frequency, arrhenius_energy, enthalpy)
    fields = flame_state.shape[0]
    grid_state = flame_state.reshape(fields, GRID_POINTS_ONE, GRID_POINTS_TWO, GRID_POINTS_THREE)
    grid_tangents = tangents.reshape(tangents.shape[0], fields, GRID_POINTS_ONE, GRID_POINTS_TWO, GRID_POINTS_THREE)
    block_cells = GRID_POINTS_TWO * GRID_POINTS_THREE
    spread = diffusivity[:, None, None, None]

    def nominal_kernel(portion):
        return nominal_chem(portion, tables)

    def nominal_rate(stored_numbers):
        chemical = blockwise(nominal_kernel, (stored_numbers.reshape(fields, -1),), block_cells)[0]
        return chemical.reshape(stored_numbers.shape) + spread * laplace(stored_numbers, 1)

    start_rate = nominal_rate(grid_state)
    middle = grid_state + time_step * start_rate
    middle_rate = nominal_rate(middle)
    new_state = grid_state + 0.5 * time_step * (start_rate + middle_rate)
    reactions = reactant_table.shape[0]

    def advance_direction(element):
        derivative_direction, chosen = element
        selection_filter = (jnp.arange(reactions, dtype=jnp.int32) == chosen).astype(jnp.float32)[None, :]

        def joint_kernel(portion, tangent_portion):
            return joint_chem(portion, tangent_portion, selection_filter, tables)

        def tangent_rate(stored_numbers, field_values):
            combined = blockwise(joint_kernel, (stored_numbers.reshape(fields, -1), field_values.reshape(1, fields, -1)), block_cells)
            return combined[1].reshape(field_values.shape) + spread * laplace(field_values, 1)

        start_change = tangent_rate(grid_state, derivative_direction)
        middle_tangent = derivative_direction + time_step * start_change
        middle_change = tangent_rate(middle, middle_tangent)
        return derivative_direction + 0.5 * time_step * (start_change + middle_change)

    new_tangents = lax.map(advance_direction, (grid_tangents, direction_index))
    return new_state.reshape(flame_state.shape), new_tangents.reshape(tangents.shape)
```

```python
import functools

import jax
import jax.numpy as jnp
from jax import lax
from jax.experimental import pallas as pl
from jax.experimental.pallas import tpu as pltpu
from jax.sharding import PartitionSpec as P

GRID_POINTS_THREE = 32
TIME_STEP = 0.2
ONE_LOW = 2.0**-10
MESH = pl.DeviceIdType.MESH
F32 = jnp.float32
BF16 = jnp.bfloat16


def in_plane(x, lane):
    cells = x.shape[1]
    width = GRID_POINTS_THREE
    before = jnp.where(
        lane == 0, pltpu.roll(x, cells - (width - 1), 1), pltpu.roll(x, 1, 1)
    )
    after = jnp.where(
        lane == width - 1, pltpu.roll(x, width - 1, 1), pltpu.roll(x, cells - 1, 1)
    )
    return before + after + (pltpu.roll(x, width, 1) + pltpu.roll(x, cells - width, 1))


def stacked(x, extra, species, row):
    base = species // 8 * 8
    tail = x[base:]
    tail = jnp.where(row == species + 1, 1.0 + ONE_LOW, jnp.where(row >= species, extra, tail))
    full = jnp.concatenate([x[:base], tail], 0)
    high = full.astype(BF16).astype(F32)
    return jnp.concatenate([high, full - high], 0).astype(BF16)


def with_heat(p, species, row, rest):
    base = species // 8 * 8
    tail = p[base:]
    heat = p[species : species + 1] + p[species + 1 : species + 2]
    tail = jnp.where(row < species, tail, jnp.where(row == species, heat, rest))
    return jnp.concatenate([p[:base], tail], 0), heat


def kernel(
    species, groups, ring,
    s_ref, t_ref, w_nominal, w_tangent, w_net, spread_ref,
    ns_ref, nt_ref,
    st, zs, mid, rates, prods, inverses, tt, mt, ns_full,
    st_send, st_recv, near_send, near_recv, far_send, far_recv, local_sem,
):
    directions = t_ref.shape[1]
    rows, cells = t_ref.shape[2], t_ref.shape[3]
    own_cells = s_ref.shape[2]
    g = lax.axis_index("grp")
    i = lax.axis_index("sp")
    odd = lax.rem(i, 2)
    partner = i + 1 - 2 * odd
    ahead = lax.rem(i + 2 - 4 * odd + ring, ring)
    behind = lax.rem(i - 2 + 4 * odd + ring, ring)
    near_side, far_side = 2 * (1 - odd), 2 * odd
    peers = [lax.rem(g + k, groups) for k in range(1, groups)]

    def remote(src, dst, send, recv, target):
        return pltpu.make_async_remote_copy(
            src_ref=src, dst_ref=dst, send_sem=send, recv_sem=recv,
            device_id=target, device_id_type=MESH,
        )

    own_t = pltpu.make_async_copy(t_ref, tt.at[pl.ds(2, 2)], local_sem.at[0])
    own_s = pltpu.make_async_copy(s_ref, st.at[1, g], local_sem.at[1])
    own_t.start()
    own_s.start()

    barrier = pltpu.get_barrier_semaphore()
    for target in [(g, partner), (g, ahead), (g, behind)] + [(p, i) for p in peers]:
        pl.semaphore_signal(barrier, inc=1, device_id=target, device_id_type=MESH)
    pl.semaphore_wait(barrier, 3 + len(peers))

    s_near = remote(s_ref, st.at[2 * odd, g], st_send.at[0], st_recv.at[2 * odd, g], (g, partner))
    s_near_in = remote(s_ref, st.at[near_side, g], st_send.at[0], st_recv.at[near_side, g], (g, partner))
    s_far = remote(st.at[near_side, g], st.at[far_side, g], st_send.at[1], st_recv.at[far_side, g], (g, ahead))

    def to_group(src, side, base):
        return [
            remote(src, st.at[side, g], st_send.at[base + k], st_recv.at[side, g], (p, i))
            for k, p in enumerate(peers)
        ]

    def near(d, p):
        return remote(
            t_ref.at[p, d], tt.at[4 * odd + p, d], near_send.at[d, p], near_recv.at[d, p], (g, partner)
        )

    def far(d, p):
        return remote(
            tt.at[4 * (1 - odd) + p, d], tt.at[4 * odd + p, d], far_send.at[d, p], far_recv.at[d, p], (g, ahead)
        )

    s_near.start()
    group_own = to_group(s_ref, 1, 2)
    for copy in group_own:
        copy.start()
    for d in range(directions):
        for p in range(2):
            near(d, p).start()

    s_near_in.wait_recv()
    s_far.start()
    group_near = to_group(st.at[near_side, g], near_side, 2 + len(peers))
    for copy in group_near:
        copy.start()
    s_far.wait_recv()
    group_far = to_group(st.at[far_side, g], far_side, 2 + 2 * len(peers))
    for copy in group_far:
        copy.start()

    def forward(d):
        for p in range(2):
            near(d, p).wait_recv()
            far(d, p).start()

    own_s.wait()
    for side in range(3):
        for p in peers:
            remote(
                st.at[side, p], st.at[side, p], st_send.at[0], st_recv.at[side, p], (p, i)
            ).wait_recv()
    for side in range(3):
        for q in range(groups):
            for p in range(2):
                zs[2 * side + p, :, q * own_cells : (q + 1) * own_cells] = st[side, q, p]
    own_t.wait()
    forward(0)

    row = lax.broadcasted_iota(jnp.int32, (rows - species // 8 * 8, cells), 0) + species // 8 * 8
    lane = lax.rem(
        lax.broadcasted_iota(jnp.int32, (rows, cells), 1), jnp.int32(GRID_POINTS_THREE)
    )
    spread = jnp.broadcast_to(spread_ref[:, :1], (rows, cells))

    def nominal(z, slot):
        level = 1.0 / z[species : species + 1]
        log_rate = jnp.dot(
            w_nominal[...], stacked(z, -level, species, row), preferred_element_type=F32
        )
        rate = jnp.exp(log_rate)
        rates[slot] = rate
        production = jnp.dot(w_net[...], rate.astype(BF16), preferred_element_type=F32)
        base = species // 8 * 8
        inverse = jnp.exp(-z)
        inverse = jnp.concatenate([inverse[:base], jnp.where(row < species, inverse[base:], 1.0)], 0)
        inverses[slot] = inverse
        plain = jnp.concatenate([production[:base], jnp.where(row < species, production[base:], 0.0)], 0)
        prods[slot] = plain
        total, _ = with_heat(production, species, row, 0.0)
        return total * inverse

    def tangent(u, level_squared, slot, d):
        change = jnp.dot(
            w_tangent[d],
            stacked(u, u[species : species + 1] * level_squared, species, row),
            preferred_element_type=F32,
        )
        moved = jnp.dot(
            w_net[...], (rates[slot] * change).astype(BF16), preferred_element_type=F32
        )
        moved, _ = with_heat(moved, species, row, 0.0)
        return (moved - prods[slot] * u) * inverses[slot]

    def squared(z):
        level = 1.0 / z[species : species + 1]
        return level * level

    def start_nominal(k, carry):
        z = zs[k + 1]
        lap = zs[k] + zs[k + 2] + in_plane(z, lane) - 6.0 * z
        rate = nominal(z, k) + spread * lap
        mid[k] = z + TIME_STEP * rate

        @pl.when((k == 1) | (k == 2))
        def _():
            ns_full[k - 1] = z + 0.5 * TIME_STEP * rate

        return carry

    lax.fori_loop(0, 4, start_nominal, 0)

    def middle_nominal(k, carry):
        z = mid[k + 1]
        lap = mid[k] + mid[k + 2] + in_plane(z, lane) - 6.0 * z
        ns_full[k] += 0.5 * TIME_STEP * (nominal(z, k + 4) + spread * lap)
        return carry

    lax.fori_loop(0, 2, middle_nominal, 0)
    for k in range(2):
        ns_ref[k] = ns_full[k, :, pl.ds(pl.multiple_of(g * own_cells, own_cells), own_cells)]

    fields = species + 1

    def direction(d, carry):
        @pl.when(d < directions - 1)
        def _():
            forward(d + 1)

        for p in range(2):
            far(d, p).wait_recv()

        def start_plane(k, carry):
            u = tt[k + 1, d]
            lap = tt[k, d] + tt[k + 2, d] + in_plane(u, lane) - 6.0 * u
            rate = tangent(u, squared(zs[k + 1]), k, d) + spread * lap
            mt[k] = u + TIME_STEP * rate

            @pl.when((k == 1) | (k == 2))
            def _():
                nt_ref[k - 1, d] = (u + 0.5 * TIME_STEP * rate)[:fields]

            return carry

        lax.fori_loop(0, 4, start_plane, 0)

        def middle_plane(k, carry):
            u = mt[k + 1]
            lap = mt[k] + mt[k + 2] + in_plane(u, lane) - 6.0 * u
            rate = tangent(u, squared(mid[k + 1]), k + 4, d) + spread * lap
            nt_ref[k, d] += (0.5 * TIME_STEP * rate)[:fields]
            return carry

        lax.fori_loop(0, 2, middle_plane, 0)
        return carry

    lax.fori_loop(0, directions, direction, 0)

    s_near.wait_send()
    s_far.wait_send()
    for copy in group_own + group_near + group_far:
        copy.wait_send()
    for d in range(directions):
        for p in range(2):
            near(d, p).wait_send()
            far(d, p).wait_send()


def split(x):
    high = lax.reduce_precision(x, 8, 7)
    return high, x - high


def shards(
    flame_state, tangents, direction_index, reactant_table, product_table,
    natural_log_frequency, arrhenius_energy, diffusivity, enthalpy,
):
    fields, planes, own_cells = flame_state.shape
    directions, cells = tangents.shape[0], tangents.shape[3]
    reactions, species = reactant_table.shape
    groups, ring = lax.axis_size("grp"), lax.axis_size("sp")
    assert planes == 2 and ring % 2 == 0
    rows = -(-(species + 3) // 8) * 8
    assert species % 8 <= 5
    depth = -(-reactions // 16) * 16

    state = jnp.pad(flame_state.transpose(1, 0, 2), ((0, 0), (0, rows - fields), (0, 0)))
    sens = jnp.pad(tangents.transpose(2, 0, 1, 3), ((0, 0), (0, 0), (0, rows - fields), (0, 0)))

    nu_in = reactant_table.astype(F32)
    nu_net = (product_table - reactant_table).astype(F32)
    e_high, e_low = split(arrhenius_energy)
    a_high, a_low = split(natural_log_frequency)
    zero = jnp.zeros((reactions, rows - species - 3), F32)

    def weights(one_high, one_low):
        def half(one):
            return [nu_in, e_high[:, None], one[:, None], e_low[:, None], zero]

        both = jnp.concatenate(half(one_high) + half(one_low), 1)
        return jnp.pad(both, ((0, depth - reactions), (0, 0))).astype(BF16)

    w_nominal = weights(a_high, a_low / ONE_LOW)
    chosen = (
        direction_index[:, None] == jnp.arange(reactions, dtype=jnp.int32)[None, :]
    ).astype(F32)
    w_tangent = jax.vmap(lambda one: weights(one, jnp.zeros_like(one)))(chosen)
    heat = -jnp.sum(nu_net * enthalpy[None, :], 1)
    h_high, h_low = split(heat)
    w_net = jnp.concatenate([nu_net, h_high[:, None], h_low[:, None]], 1).T
    w_net = jnp.pad(w_net, ((0, rows - species - 2), (0, depth - reactions))).astype(BF16)
    spread = jnp.broadcast_to(jnp.pad(diffusivity, (0, rows - fields))[:, None], (rows, 128))

    vmem = pl.BlockSpec(memory_space=pltpu.VMEM)
    anywhere = pl.BlockSpec(memory_space=pl.ANY)
    new_state, new_sens = pl.pallas_call(
        functools.partial(kernel, species, groups, ring),
        out_shape=(
            jax.ShapeDtypeStruct((2, rows, own_cells), F32),
            jax.ShapeDtypeStruct((2, directions, fields, cells), F32),
        ),
        in_specs=[anywhere, anywhere, vmem, vmem, vmem, vmem],
        out_specs=(vmem, vmem),
        scratch_shapes=[
            pltpu.VMEM((3, groups, 2, rows, own_cells), F32),
            pltpu.VMEM((6, rows, cells), F32),
            pltpu.VMEM((4, rows, cells), F32),
            pltpu.VMEM((6, depth, cells), F32),
            pltpu.VMEM((6, rows, cells), F32),
            pltpu.VMEM((6, rows, cells), F32),
            pltpu.VMEM((6, directions, rows, cells), F32),
            pltpu.VMEM((4, rows, cells), F32),
            pltpu.VMEM((2, rows, cells), F32),
            pltpu.SemaphoreType.DMA((2 + 3 * (groups - 1),)),
            pltpu.SemaphoreType.DMA((3, groups)),
            pltpu.SemaphoreType.DMA((directions, 2)),
            pltpu.SemaphoreType.DMA((directions, 2)),
            pltpu.SemaphoreType.DMA((directions, 2)),
            pltpu.SemaphoreType.DMA((directions, 2)),
            pltpu.SemaphoreType.DMA((2,)),
        ],
        compiler_params=pltpu.CompilerParams(
            collective_id=0, has_side_effects=True, vmem_limit_bytes=48 << 20
        ),
        name="step",
    )(state, sens, w_nominal, w_tangent, w_net, spread)
    return (
        new_state[:, :fields].transpose(1, 0, 2),
        new_sens.transpose(1, 2, 0, 3),
    )


def solution(mesh):
    in_specs = (
        P(None, "sp", "grp"), P("grp", None, "sp", None), P("grp"),
        P(), P(), P(), P(), P(), P(),
    )
    out_specs = (P(None, "sp", "grp"), P("grp", None, "sp", None))
    return jax.shard_map(shards, mesh=mesh, in_specs=in_specs, out_specs=out_specs, check_vma=False)
```

```python
import functools

import jax
import jax.numpy as jnp
from jax import lax
from jax.experimental import pallas as pl
from jax.experimental.pallas import tpu as pltpu
from jax.sharding import PartitionSpec as P

GRID_POINTS_THREE = 32
TIME_STEP = 0.2
ONE_LOW = 2.0**-10
MESH = pl.DeviceIdType.MESH
F32 = jnp.float32
BF16 = jnp.bfloat16


def in_plane(x, lane):
    cells = x.shape[1]
    width = GRID_POINTS_THREE
    before = jnp.where(
        lane == 0, pltpu.roll(x, cells - (width - 1), 1), pltpu.roll(x, 1, 1)
    )
    after = jnp.where(
        lane == width - 1, pltpu.roll(x, width - 1, 1), pltpu.roll(x, cells - 1, 1)
    )
    return before + after + (pltpu.roll(x, width, 1) + pltpu.roll(x, cells - width, 1))


def stacked(x, extra, species, row):
    base = species // 8 * 8
    tail = x[base:]
    tail = jnp.where(row == species + 1, 1.0 + ONE_LOW, jnp.where(row >= species, extra, tail))
    full = jnp.concatenate([x[:base], tail], 0)
    high = full.astype(BF16).astype(F32)
    return jnp.concatenate([high, full - high], 0).astype(BF16)


def halves(x):
    high = x.astype(BF16).astype(F32)
    return high, x - high


def with_heat(p, species, row):
    base = species // 8 * 8
    tail = p[base:]
    heat = p[species : species + 1] + p[species + 1 : species + 2]
    tail = jnp.where(row < species, tail, jnp.where(row == species, heat, 0.0))
    return jnp.concatenate([p[:base], tail], 0)


def column(vector, rows):
    count = vector.shape[0]
    wide = jnp.broadcast_to(vector.reshape(1, count), (rows, count))
    diagonal = lax.broadcasted_iota(jnp.int32, (rows, count), 0) == lax.broadcasted_iota(
        jnp.int32, (rows, count), 1
    )
    return jnp.sum(jnp.where(diagonal, wide, 0.0), axis=1, keepdims=True)


def build_weights(
    species, directions, react, product, lna, energy, diffus, enthalpy, index,
    w_nominal, w_tangent, w_net, spread, wide, flat,
):
    rows = w_net.shape[0]
    reactions = react.shape[1]
    depth = w_nominal.shape[0]
    nu_in = react[...].astype(F32)
    nu_net = (product[...] - react[...]).astype(F32)
    e_high, e_low = halves(energy[...].reshape(1, reactions))
    a_high, a_low = halves(lna[...].reshape(1, reactions))
    wide[...] = jnp.zeros_like(wide)
    for base, one in ((0, a_high), (rows, a_low * (1.0 / ONE_LOW))):
        wide[base : base + species, :reactions] = nu_in
        wide[base + species : base + species + 1, :reactions] = e_high
        wide[base + species + 1 : base + species + 2, :reactions] = one
        wide[base + species + 2 : base + species + 3, :reactions] = e_low
    nominal = jnp.transpose(wide[...])[:depth]
    w_nominal[...] = nominal.astype(BF16)
    reaction = lax.broadcasted_iota(jnp.int32, nominal.shape, 0)
    place = lax.broadcasted_iota(jnp.int32, nominal.shape, 1)
    cleared = jnp.where(
        (place == species + 1) | (place == rows + species + 1), 0.0, nominal
    )
    for d in range(directions):
        chosen = (reaction == index[d]) & (place == species + 1)
        w_tangent[d] = jnp.where(chosen, 1.0, cleared).astype(BF16)
    heat = -jnp.sum(nu_net * column(enthalpy[...], species), axis=0, keepdims=True)
    h_high, h_low = halves(heat)
    flat[...] = jnp.zeros_like(flat)
    flat[:species, :reactions] = nu_net
    flat[species : species + 1, :reactions] = h_high
    flat[species + 1 : species + 2, :reactions] = h_low
    w_net[...] = flat[...][:, :depth].astype(BF16)
    spread[...] = jnp.broadcast_to(column(diffus[...], rows), spread.shape)


def kernel(
    species, groups, ring,
    s_ref, t_ref, react_hbm, product_hbm, lna_hbm, energy_hbm, diffus_hbm, enthalpy_hbm, index,
    ns_ref, nt_ref,
    react, product, lna, energy, diffus, enthalpy,
    w_nominal, w_tangent, w_net, spread_ref, wide, flat,
    st, zs, mid, rates, prods, inverses, tt, mt, part, ns_full,
    st_send, st_recv, near_send, near_recv, far_send, far_recv, local_sem,
):
    directions = t_ref.shape[1]
    rows, cells = t_ref.shape[2], t_ref.shape[3]
    half = cells // 2
    own_cells = s_ref.shape[2]
    fields = species + 1
    base = species // 8 * 8
    g = lax.axis_index("grp")
    i = lax.axis_index("sp")
    odd = lax.rem(i, 2)
    partner = i + 1 - 2 * odd
    ahead = lax.rem(i + 2 - 4 * odd + ring, ring)
    behind = lax.rem(i - 2 + 4 * odd + ring, ring)
    near_side, far_side = 2 * (1 - odd), 2 * odd
    near_k, far_k = 3 * (1 - odd), 3 * odd
    peers = [lax.rem(g + k, groups) for k in range(1, groups)]

    def remote(src, dst, send, recv, target):
        return pltpu.make_async_remote_copy(
            src_ref=src, dst_ref=dst, send_sem=send, recv_sem=recv,
            device_id=target, device_id_type=MESH,
        )

    locals_ = [
        pltpu.make_async_copy(src, dst, local_sem.at[n])
        for n, (src, dst) in enumerate(
            [
                (t_ref, tt.at[pl.ds(2, 2)]), (s_ref, st.at[1, g]), (react_hbm, react),
                (product_hbm, product), (lna_hbm, lna), (energy_hbm, energy),
                (diffus_hbm, diffus), (enthalpy_hbm, enthalpy),
            ]
        )
    ]
    for copy in locals_[2:]:
        copy.start()

    barrier = pltpu.get_barrier_semaphore()
    for target in [(g, partner), (g, ahead), (g, behind)] + [(p, i) for p in peers]:
        pl.semaphore_signal(barrier, inc=1, device_id=target, device_id_type=MESH)
    for copy in locals_[:2]:
        copy.start()
    pl.semaphore_wait(barrier, 3 + len(peers))

    s_near = remote(s_ref, st.at[2 * odd, g], st_send.at[0], st_recv.at[2 * odd, g], (g, partner))
    s_near_in = remote(s_ref, st.at[near_side, g], st_send.at[0], st_recv.at[near_side, g], (g, partner))
    s_far = remote(st.at[near_side, g], st.at[far_side, g], st_send.at[1], st_recv.at[far_side, g], (g, ahead))

    def to_group(src, side, first):
        return [
            remote(src, st.at[side, g], st_send.at[first + k], st_recv.at[side, g], (p, i))
            for k, p in enumerate(peers)
        ]

    def piece(c):
        return c // 4, lax.rem(c // 2, 2), lax.rem(c, 2)

    def window(buffer, plane, d, h):
        return buffer.at[plane, d, :, pl.ds(pl.multiple_of(h * half, half), half)]

    def near(c):
        d, p, h = piece(c)
        return remote(
            window(t_ref, p, d, h), window(tt, 4 * odd + p, d, h),
            near_send.at[c], near_recv.at[c], (g, partner),
        )

    def far(c):
        d, p, h = piece(c)
        return remote(
            window(tt, 4 * (1 - odd) + p, d, h), window(tt, 4 * odd + p, d, h),
            far_send.at[c], far_recv.at[c], (g, ahead),
        )

    pieces = 4 * directions

    def forward(c):
        near(c).wait_recv()
        far(c).start()

    def span(low, high, step):
        lax.fori_loop(low, high, lambda c, carry: (step(c), carry)[1], 0)

    s_near.start()
    group_own = to_group(s_ref, 1, 2)
    for copy in group_own:
        copy.start()
    span(0, pieces, lambda c: near(c).start())

    for copy in locals_[2:]:
        copy.wait()
    build_weights(
        species, directions, react, product, lna, energy, diffus, enthalpy, index,
        w_nominal, w_tangent, w_net, spread_ref, wide, flat,
    )
    row = lax.broadcasted_iota(jnp.int32, (rows - base, cells), 0) + base
    lane = lax.rem(
        lax.broadcasted_iota(jnp.int32, (rows, cells), 1), jnp.int32(GRID_POINTS_THREE)
    )

    def arrived(side):
        for p in peers:
            remote(
                st.at[side, p], st.at[side, p], st_send.at[0], st_recv.at[side, p], (p, i)
            ).wait_recv()
        for q in range(groups):
            for p in range(2):
                zs[2 * side + p, :, q * own_cells : (q + 1) * own_cells] = st[side, q, p]

    def nominal(z, slot):
        level = 1.0 / z[species : species + 1]
        rate = jnp.exp(
            jnp.dot(
                w_nominal[...], stacked(z, -level, species, row), preferred_element_type=F32
            )
        )
        rates[slot] = rate
        high, low = halves(rate)
        production = jnp.dot(
            w_net[...], high.astype(BF16), preferred_element_type=F32
        ) + jnp.dot(w_net[...], low.astype(BF16), preferred_element_type=F32)
        inverse = jnp.exp(-z)
        inverse = jnp.concatenate([inverse[:base], jnp.where(row < species, inverse[base:], 1.0)], 0)
        inverses[slot] = inverse
        prods[slot] = jnp.concatenate(
            [production[:base], jnp.where(row < species, production[base:], 0.0)], 0
        )
        return with_heat(production, species, row) * inverse

    def tangent(u, z, slot, d):
        level = 1.0 / z[species : species + 1]
        change = jnp.dot(
            w_tangent[d],
            stacked(u, u[species : species + 1] * (level * level), species, row),
            preferred_element_type=F32,
        )
        moved = jnp.dot(
            w_net[...], (rates[slot] * change).astype(BF16), preferred_element_type=F32
        )
        return (with_heat(moved, species, row) - prods[slot] * u) * inverses[slot]

    def lap(low, x, high):
        return low + high + in_plane(x, lane) - 6.0 * x

    s_near_in.wait_recv()
    s_far.start()
    group_near = to_group(st.at[near_side, g], near_side, 2 + len(peers))
    for copy in group_near:
        copy.start()
    locals_[1].wait()
    arrived(1)
    for k in (1, 2):
        mid[k] = nominal(zs[k + 1], k)
    locals_[0].wait()
    span(0, 2, forward)
    s_far.wait_recv()
    group_far = to_group(st.at[far_side, g], far_side, 2 + 2 * len(peers))
    for copy in group_far:
        copy.start()
    span(2, 3, forward)

    def own_planes(d, carry):
        spread = spread_ref[...]
        for k in (1, 2):
            u = tt[k + 1, d]
            inner = tt[4 - k, d] + in_plane(u, lane) - 6.0 * u
            part[d, k - 1] = tangent(u, zs[k + 1], k, d) + spread * inner
        forward(3 + d)
        return carry

    lax.fori_loop(0, directions, own_planes, 0)
    done = 3 + directions

    arrived(near_side)
    mid[near_k] = nominal(zs[near_k + 1], near_k)
    span(done, done + 1, forward)
    arrived(far_side)
    mid[far_k] = nominal(zs[far_k + 1], far_k)
    for k in range(4):
        z = zs[k + 1]
        rate = mid[k] + spread_ref[...] * lap(zs[k], z, zs[k + 2])
        mid[k] = z + TIME_STEP * rate
        if k in (1, 2):
            ns_full[k - 1] = z + 0.5 * TIME_STEP * rate
    span(done + 1, done + 2, forward)
    for k in (1, 2):
        z = mid[k]
        rate = nominal(z, k + 3) + spread_ref[...] * lap(mid[k - 1], z, mid[k + 1])
        ns_full[k - 1] += 0.5 * TIME_STEP * rate
    for k in range(2):
        ns_ref[k] = ns_full[k, :, pl.ds(pl.multiple_of(g * own_cells, own_cells), own_cells)]
    span(done + 2, 4 * (directions - 1), forward)

    def halo(k, d):
        u = tt[k + 1, d]
        rate = tangent(u, zs[k + 1], k, d) + spread_ref[...] * lap(tt[k, d], u, tt[k + 2, d])
        mt[k] = u + TIME_STEP * rate

    def direction(d, carry):
        @pl.when(d == directions - 2)
        def _():
            span(4 * (directions - 1), pieces, forward)

        halo(near_k, d)
        span(4 * d, 4 * d + 4, lambda c: far(c).wait_recv())
        spread = spread_ref[...]
        halo(far_k, d)
        for k in (1, 2):
            u = tt[k + 1, d]
            rate = part[d, k - 1] + spread * tt[3 * k - 2, d]
            mt[k] = u + TIME_STEP * rate
            part[d, k - 1] = u + 0.5 * TIME_STEP * rate
        for k in (1, 2):
            u = mt[k]
            rate = tangent(u, mid[k], k + 3, d) + spread * lap(mt[k - 1], u, mt[k + 1])
            nt_ref[k - 1, d] = (part[d, k - 1] + 0.5 * TIME_STEP * rate)[:fields]
        return carry

    lax.fori_loop(0, directions, direction, 0)

    s_near.wait_send()
    s_far.wait_send()
    for copy in group_own + group_near + group_far:
        copy.wait_send()

    def sent(c):
        near(c).wait_send()
        far(c).wait_send()

    span(0, pieces, sent)


def shards(
    flame_state, tangents, direction_index, reactant_table, product_table,
    natural_log_frequency, arrhenius_energy, diffusivity, enthalpy,
):
    fields, planes, own_cells = flame_state.shape
    directions, cells = tangents.shape[0], tangents.shape[3]
    reactions, species = reactant_table.shape
    groups, ring = lax.axis_size("grp"), lax.axis_size("sp")
    assert planes == 2 and ring % 2 == 0 and directions >= 3
    rows = -(-(species + 3) // 8) * 8
    assert species % 8 <= 5
    depth = -(-reactions // 16) * 16
    lanes = -(-reactions // 128) * 128

    state = jnp.pad(flame_state.transpose(1, 0, 2), ((0, 0), (0, rows - fields), (0, 0)))
    sens = jnp.pad(tangents.transpose(2, 0, 1, 3), ((0, 0), (0, 0), (0, rows - fields), (0, 0)))

    vmem = pl.BlockSpec(memory_space=pltpu.VMEM)
    anywhere = pl.BlockSpec(memory_space=pl.ANY)
    hbm = pl.BlockSpec(memory_space=pltpu.HBM)
    smem = pl.BlockSpec(memory_space=pltpu.SMEM)
    pieces = 4 * directions
    new_state, new_sens = pl.pallas_call(
        functools.partial(kernel, species, groups, ring),
        out_shape=(
            jax.ShapeDtypeStruct((2, rows, own_cells), F32),
            jax.ShapeDtypeStruct((2, directions, fields, cells), F32),
        ),
        in_specs=[anywhere, anywhere] + [hbm] * 6 + [smem],
        out_specs=(vmem, vmem),
        scratch_shapes=[
            pltpu.VMEM((species, reactions), jnp.int32),
            pltpu.VMEM((species, reactions), jnp.int32),
            pltpu.VMEM((reactions,), F32),
            pltpu.VMEM((reactions,), F32),
            pltpu.VMEM((fields,), F32),
            pltpu.VMEM((species,), F32),
            pltpu.VMEM((depth, 2 * rows), BF16),
            pltpu.VMEM((directions, depth, 2 * rows), BF16),
            pltpu.VMEM((rows, depth), BF16),
            pltpu.VMEM((rows, cells), F32),
            pltpu.VMEM((2 * rows, lanes), F32),
            pltpu.VMEM((rows, lanes), F32),
            pltpu.VMEM((3, groups, 2, rows, own_cells), F32),
            pltpu.VMEM((6, rows, cells), F32),
            pltpu.VMEM((4, rows, cells), F32),
            pltpu.VMEM((6, depth, cells), F32),
            pltpu.VMEM((6, rows, cells), F32),
            pltpu.VMEM((6, rows, cells), F32),
            pltpu.VMEM((6, directions, rows, cells), F32),
            pltpu.VMEM((4, rows, cells), F32),
            pltpu.VMEM((directions, 2, rows, cells), F32),
            pltpu.VMEM((2, rows, cells), F32),
            pltpu.SemaphoreType.DMA((2 + 3 * (groups - 1),)),
            pltpu.SemaphoreType.DMA((3, groups)),
            pltpu.SemaphoreType.DMA((pieces,)),
            pltpu.SemaphoreType.DMA((pieces,)),
            pltpu.SemaphoreType.DMA((pieces,)),
            pltpu.SemaphoreType.DMA((pieces,)),
            pltpu.SemaphoreType.DMA((8,)),
        ],
        compiler_params=pltpu.CompilerParams(
            collective_id=0, has_side_effects=True, vmem_limit_bytes=48 << 20
        ),
        name="step",
    )(
        state, sens, reactant_table.T, product_table.T, natural_log_frequency,
        arrhenius_energy, diffusivity, enthalpy, direction_index,
    )
    return (
        new_state[:, :fields].transpose(1, 0, 2),
        new_sens.transpose(1, 2, 0, 3),
    )


def solution(mesh):
    in_specs = (
        P(None, "sp", "grp"), P("grp", None, "sp", None), P("grp"),
        P(), P(), P(), P(), P(), P(),
    )
    out_specs = (P(None, "sp", "grp"), P("grp", None, "sp", None))
    return jax.shard_map(shards, mesh=mesh, in_specs=in_specs, out_specs=out_specs, check_vma=False)
```

```python
import functools
import math

import jax
import jax.numpy as jnp
from jax import lax
from jax.experimental import pallas as pl
from jax.experimental.pallas import tpu as pltpu
from jax.sharding import PartitionSpec as P

GRID_POINTS_THREE = 32
TIME_STEP = 0.2
ONE_LOW = 2.0**-10
MESH = pl.DeviceIdType.MESH
F32 = jnp.float32
BF16 = jnp.bfloat16


def in_plane(x, lane):
    cells = x.shape[1]
    width = GRID_POINTS_THREE
    before = jnp.where(
        lane == 0, pltpu.roll(x, cells - (width - 1), 1), pltpu.roll(x, 1, 1)
    )
    after = jnp.where(
        lane == width - 1, pltpu.roll(x, width - 1, 1), pltpu.roll(x, cells - 1, 1)
    )
    return before + after + (pltpu.roll(x, width, 1) + pltpu.roll(x, cells - width, 1))


def stacked(x, extra, species, row):
    base = species // 8 * 8
    tail = x[base:]
    tail = jnp.where(row == species + 1, 1.0 + ONE_LOW, jnp.where(row >= species, extra, tail))
    full = jnp.concatenate([x[:base], tail], 0)
    high = full.astype(BF16).astype(F32)
    return jnp.concatenate([high, full - high], 0).astype(BF16)


def halves(x):
    high = x.astype(BF16).astype(F32)
    return high, x - high


def with_heat(p, species, row):
    base = species // 8 * 8
    tail = p[base:]
    heat = p[species : species + 1] + p[species + 1 : species + 2]
    tail = jnp.where(row < species, tail, jnp.where(row == species, heat, 0.0))
    return jnp.concatenate([p[:base], tail], 0)


def column(vector, rows):
    count = vector.shape[0]
    wide = jnp.broadcast_to(vector.reshape(1, count), (rows, count))
    diagonal = lax.broadcasted_iota(jnp.int32, (rows, count), 0) == lax.broadcasted_iota(
        jnp.int32, (rows, count), 1
    )
    return jnp.sum(jnp.where(diagonal, wide, 0.0), axis=1, keepdims=True)


def build_weights(
    species, directions, react, product, lna, energy, diffus, enthalpy, index,
    w_nominal, w_tangent, w_net, spread, wide, flat,
):
    rows = w_net.shape[0]
    reactions = react.shape[1]
    depth = w_nominal.shape[0]
    nu_in = react[...].astype(F32)
    nu_net = (product[...] - react[...]).astype(F32)
    e_high, e_low = halves(energy[...].reshape(1, reactions))
    a_high, a_low = halves(lna[...].reshape(1, reactions))
    wide[...] = jnp.zeros_like(wide)
    for base, one in ((0, a_high), (rows, a_low * (1.0 / ONE_LOW))):
        wide[base : base + species, :reactions] = nu_in
        wide[base + species : base + species + 1, :reactions] = e_high
        wide[base + species + 1 : base + species + 2, :reactions] = one
        wide[base + species + 2 : base + species + 3, :reactions] = e_low
    nominal = jnp.transpose(wide[...])[:depth]
    w_nominal[...] = nominal.astype(BF16)
    reaction = lax.broadcasted_iota(jnp.int32, nominal.shape, 0)
    place = lax.broadcasted_iota(jnp.int32, nominal.shape, 1)
    cleared = jnp.where(
        (place == species + 1) | (place == rows + species + 1), 0.0, nominal
    )
    for d in range(directions):
        chosen = (reaction == index[d]) & (place == species + 1)
        w_tangent[d] = jnp.where(chosen, 1.0, cleared).astype(BF16)
    heat = -jnp.sum(nu_net * column(enthalpy[...], species), axis=0, keepdims=True)
    h_high, h_low = halves(heat)
    flat[...] = jnp.zeros_like(flat)
    flat[:species, :reactions] = nu_net
    flat[species : species + 1, :reactions] = h_high
    flat[species + 1 : species + 2, :reactions] = h_low
    w_net[...] = flat[...][:, :depth].astype(BF16)
    spread[...] = jnp.broadcast_to(column(diffus[...], rows), spread.shape)


def kernel(
    species, groups, ring,
    s_ref, t_ref, react_hbm, product_hbm, lna_hbm, energy_hbm, diffus_hbm, enthalpy_hbm, index,
    ns_ref, nt_ref,
    react, product, lna, energy, diffus, enthalpy,
    w_nominal, w_tangent, w_net, spread_ref, wide, flat,
    raw, st, zs, mid, rates, prods, inverses, tt, mt, part, ns_full,
    st_send, st_recv, near_send, near_recv, far_send, far_recv, local_sem,
):
    directions = t_ref.shape[0]
    rows, cells = w_net.shape[0], zs.shape[2]
    own_cells = s_ref.shape[2]
    fields = species + 1
    base = species // 8 * 8
    cuts = near_send.shape[0] // directions
    g = lax.axis_index("grp")
    i = lax.axis_index("sp")
    odd = lax.rem(i, 2)
    partner = i + 1 - 2 * odd
    ahead = lax.rem(i + 2 - 4 * odd + ring, ring)
    behind = lax.rem(i - 2 + 4 * odd + ring, ring)
    near_side, far_side = 2 * (1 - odd), 2 * odd
    near_k, far_k = 3 * (1 - odd), 3 * odd
    peers = [lax.rem(g + k, groups) for k in range(1, groups)]

    def remote(src, dst, send, recv, target):
        return pltpu.make_async_remote_copy(
            src_ref=src, dst_ref=dst, send_sem=send, recv_sem=recv,
            device_id=target, device_id_type=MESH,
        )

    locals_ = [
        pltpu.make_async_copy(src, dst, local_sem.at[n])
        for n, (src, dst) in enumerate(
            [
                (t_ref, raw.at[1]), (s_ref, st.at[1, g]), (react_hbm, react),
                (product_hbm, product), (lna_hbm, lna), (energy_hbm, energy),
                (diffus_hbm, diffus), (enthalpy_hbm, enthalpy),
            ]
        )
    ]
    for copy in locals_[2:]:
        copy.start()

    barrier = pltpu.get_barrier_semaphore()
    for target in [(g, partner), (g, ahead), (g, behind)] + [(p, i) for p in peers]:
        pl.semaphore_signal(barrier, inc=1, device_id=target, device_id_type=MESH)
    for copy in locals_[:2]:
        copy.start()
    pl.semaphore_wait(barrier, 3 + len(peers))

    s_near = remote(s_ref, st.at[2 * odd, g], st_send.at[0], st_recv.at[2 * odd, g], (g, partner))
    s_near_in = remote(s_ref, st.at[near_side, g], st_send.at[0], st_recv.at[near_side, g], (g, partner))
    s_far = remote(st.at[near_side, g], st.at[far_side, g], st_send.at[1], st_recv.at[far_side, g], (g, ahead))

    def to_group(src, side, first):
        return [
            remote(src, st.at[side, g], st_send.at[first + k], st_recv.at[side, g], (p, i))
            for k, p in enumerate(peers)
        ]

    def window(buffer, c):
        d, h = c // cuts, lax.rem(c, cuts)
        return buffer.at[d, pl.ds(h * (fields // cuts), fields // cuts)]

    def near(c):
        return remote(
            window(t_ref, c), window(raw.at[2 * odd], c), near_send.at[c], near_recv.at[c], (g, partner)
        )

    def far(c):
        return remote(
            window(raw.at[near_side], c), window(raw.at[far_side], c),
            far_send.at[c], far_recv.at[c], (g, ahead),
        )

    def unpack(side, d):
        block = raw[side, d]
        block = jnp.concatenate([block, jnp.zeros((rows - fields,) + block.shape[1:], F32)], 0)
        block = jnp.swapaxes(block, 0, 1)
        for q in range(block.shape[0]):
            lanes = block.shape[2]
            tt[2 * side + q % 2, d, :, q // 2 * lanes : (q // 2 + 1) * lanes] = block[q]

    pieces = cuts * directions

    def forward(c):
        near(c).wait_recv()
        far(c).start()

    def span(low, high, step):
        lax.fori_loop(low, high, lambda c, carry: (step(c), carry)[1], 0)

    s_near.start()
    group_own = to_group(s_ref, 1, 2)
    for copy in group_own:
        copy.start()
    span(0, pieces, lambda c: near(c).start())

    for copy in locals_[2:]:
        copy.wait()
    build_weights(
        species, directions, react, product, lna, energy, diffus, enthalpy, index,
        w_nominal, w_tangent, w_net, spread_ref, wide, flat,
    )
    row = lax.broadcasted_iota(jnp.int32, (rows - base, cells), 0) + base
    lane = lax.rem(
        lax.broadcasted_iota(jnp.int32, (rows, cells), 1), jnp.int32(GRID_POINTS_THREE)
    )

    def arrived(side):
        for p in peers:
            remote(
                st.at[side, p], st.at[side, p], st_send.at[0], st_recv.at[side, p], (p, i)
            ).wait_recv()
        for q in range(groups):
            slab = st[side, q]
            slab = jnp.concatenate([slab, jnp.zeros((rows - fields,) + slab.shape[1:], F32)], 0)
            slab = jnp.swapaxes(slab, 0, 1)
            for p in range(2):
                zs[2 * side + p, :, q * own_cells : (q + 1) * own_cells] = slab[p]

    def nominal(z, slot):
        level = 1.0 / z[species : species + 1]
        rate = jnp.exp(
            jnp.dot(
                w_nominal[...], stacked(z, -level, species, row), preferred_element_type=F32
            )
        )
        rates[slot] = rate
        high, low = halves(rate)
        production = jnp.dot(
            w_net[...], high.astype(BF16), preferred_element_type=F32
        ) + jnp.dot(w_net[...], low.astype(BF16), preferred_element_type=F32)
        inverse = jnp.exp(-z)
        inverse = jnp.concatenate([inverse[:base], jnp.where(row < species, inverse[base:], 1.0)], 0)
        inverses[slot] = inverse
        prods[slot] = jnp.concatenate(
            [production[:base], jnp.where(row < species, production[base:], 0.0)], 0
        )
        return with_heat(production, species, row) * inverse

    def tangent(u, z, slot, d):
        level = 1.0 / z[species : species + 1]
        change = jnp.dot(
            w_tangent[d],
            stacked(u, u[species : species + 1] * (level * level), species, row),
            preferred_element_type=F32,
        )
        moved = jnp.dot(
            w_net[...], (rates[slot] * change).astype(BF16), preferred_element_type=F32
        )
        return (with_heat(moved, species, row) - prods[slot] * u) * inverses[slot]

    def lap(low, x, high):
        return low + high + in_plane(x, lane) - 6.0 * x

    s_near_in.wait_recv()
    s_far.start()
    group_near = to_group(st.at[near_side, g], near_side, 2 + len(peers))
    for copy in group_near:
        copy.start()
    locals_[1].wait()
    arrived(1)
    for k in (1, 2):
        mid[k] = nominal(zs[k + 1], k)
    locals_[0].wait()
    span(0, cuts // 2, forward)
    s_far.wait_recv()
    group_far = to_group(st.at[far_side, g], far_side, 2 + 2 * len(peers))
    for copy in group_far:
        copy.start()
    span(cuts // 2, cuts, forward)

    def own_planes(d, carry):
        spread = spread_ref[...]
        unpack(1, d)
        for k in (1, 2):
            u = tt[k + 1, d]
            inner = tt[4 - k, d] + in_plane(u, lane) - 6.0 * u
            part[d, k - 1] = tangent(u, zs[k + 1], k, d) + spread * inner
        forward(cuts + d)
        return carry

    lax.fori_loop(0, directions, own_planes, 0)
    done = cuts + directions

    arrived(near_side)
    mid[near_k] = nominal(zs[near_k + 1], near_k)
    span(done, done + 1, forward)
    arrived(far_side)
    mid[far_k] = nominal(zs[far_k + 1], far_k)
    for k in range(4):
        z = zs[k + 1]
        rate = mid[k] + spread_ref[...] * lap(zs[k], z, zs[k + 2])
        mid[k] = z + TIME_STEP * rate
        if k in (1, 2):
            ns_full[k - 1] = z + 0.5 * TIME_STEP * rate
    span(done + 1, done + 2, forward)
    for k in (1, 2):
        z = mid[k]
        rate = nominal(z, k + 3) + spread_ref[...] * lap(mid[k - 1], z, mid[k + 1])
        ns_full[k - 1] += 0.5 * TIME_STEP * rate
    own = pl.ds(pl.multiple_of(g * own_cells, own_cells), own_cells)
    ns_ref[...] = jnp.swapaxes(ns_full[:, :, own], 0, 1)[:fields]
    span(done + 2, cuts * (directions - 1), forward)

    def halo(k, d):
        u = tt[k + 1, d]
        rate = tangent(u, zs[k + 1], k, d) + spread_ref[...] * lap(tt[k, d], u, tt[k + 2, d])
        mt[k] = u + TIME_STEP * rate

    def direction(d, carry):
        @pl.when(d == directions - 2)
        def _():
            span(cuts * (directions - 1), pieces, forward)

        unpack(near_side, d)
        halo(near_k, d)
        span(cuts * d, cuts * d + cuts, lambda c: far(c).wait_recv())
        unpack(far_side, d)
        spread = spread_ref[...]
        halo(far_k, d)
        for k in (1, 2):
            u = tt[k + 1, d]
            rate = part[d, k - 1] + spread * tt[3 * k - 2, d]
            mt[k] = u + TIME_STEP * rate
            part[d, k - 1] = u + 0.5 * TIME_STEP * rate
        for k in (1, 2):
            u = mt[k]
            rate = tangent(u, mid[k], k + 3, d) + spread * lap(mt[k - 1], u, mt[k + 1])
            part[d, k - 1] += 0.5 * TIME_STEP * rate
        lanes = t_ref.shape[3]
        tiles = [
            part[d, p, :, q * lanes : (q + 1) * lanes] for q in range(cells // lanes) for p in range(2)
        ]
        nt_ref[d] = jnp.swapaxes(jnp.stack(tiles, 0), 0, 1)[:fields]
        return carry

    lax.fori_loop(0, directions, direction, 0)

    s_near.wait_send()
    s_far.wait_send()
    for copy in group_own + group_near + group_far:
        copy.wait_send()

    def sent(c):
        near(c).wait_send()
        far(c).wait_send()

    span(0, pieces, sent)


def shards(
    flame_state, tangents, direction_index, reactant_table, product_table,
    natural_log_frequency, arrhenius_energy, diffusivity, enthalpy,
):
    fields, planes, own_cells = flame_state.shape
    directions, cells = tangents.shape[0], tangents.shape[3]
    reactions, species = reactant_table.shape
    groups, ring = lax.axis_size("grp"), lax.axis_size("sp")
    assert planes == 2 and ring % 2 == 0 and directions >= 3
    rows = -(-(species + 3) // 8) * 8
    assert species % 8 <= 5
    depth = -(-reactions // 16) * 16
    lanes = -(-reactions // 128) * 128
    tile = math.gcd(cells, 128)

    sens = tangents.reshape(directions, fields, planes, cells // tile, tile).transpose(0, 1, 3, 2, 4)
    sens = sens.reshape(directions, fields, planes * cells // tile, tile)

    vmem = pl.BlockSpec(memory_space=pltpu.VMEM)
    anywhere = pl.BlockSpec(memory_space=pl.ANY)
    hbm = pl.BlockSpec(memory_space=pltpu.HBM)
    smem = pl.BlockSpec(memory_space=pltpu.SMEM)
    pieces = math.gcd(fields, 6) * directions
    new_state, new_sens = pl.pallas_call(
        functools.partial(kernel, species, groups, ring),
        out_shape=(
            jax.ShapeDtypeStruct(flame_state.shape, F32),
            jax.ShapeDtypeStruct(sens.shape, F32),
        ),
        in_specs=[anywhere, anywhere] + [hbm] * 6 + [smem],
        out_specs=(vmem, vmem),
        scratch_shapes=[
            pltpu.VMEM((species, reactions), jnp.int32),
            pltpu.VMEM((species, reactions), jnp.int32),
            pltpu.VMEM((reactions,), F32),
            pltpu.VMEM((reactions,), F32),
            pltpu.VMEM((fields,), F32),
            pltpu.VMEM((species,), F32),
            pltpu.VMEM((depth, 2 * rows), BF16),
            pltpu.VMEM((directions, depth, 2 * rows), BF16),
            pltpu.VMEM((rows, depth), BF16),
            pltpu.VMEM((rows, cells), F32),
            pltpu.VMEM((2 * rows, lanes), F32),
            pltpu.VMEM((rows, lanes), F32),
            pltpu.VMEM((3,) + sens.shape, F32),
            pltpu.VMEM((3, groups) + flame_state.shape, F32),
            pltpu.VMEM((6, rows, cells), F32),
            pltpu.VMEM((4, rows, cells), F32),
            pltpu.VMEM((6, depth, cells), F32),
            pltpu.VMEM((6, rows, cells), F32),
            pltpu.VMEM((6, rows, cells), F32),
            pltpu.VMEM((6, directions, rows, cells), F32),
            pltpu.VMEM((4, rows, cells), F32),
            pltpu.VMEM((directions, 2, rows, cells), F32),
            pltpu.VMEM((2, rows, cells), F32),
            pltpu.SemaphoreType.DMA((2 + 3 * (groups - 1),)),
            pltpu.SemaphoreType.DMA((3, groups)),
            pltpu.SemaphoreType.DMA((pieces,)),
            pltpu.SemaphoreType.DMA((pieces,)),
            pltpu.SemaphoreType.DMA((pieces,)),
            pltpu.SemaphoreType.DMA((pieces,)),
            pltpu.SemaphoreType.DMA((8,)),
        ],
        compiler_params=pltpu.CompilerParams(
            collective_id=0, has_side_effects=True, vmem_limit_bytes=48 << 20
        ),
        name="step",
    )(
        flame_state, sens, reactant_table.T, product_table.T, natural_log_frequency,
        arrhenius_energy, diffusivity, enthalpy, direction_index,
    )
    new_sens = new_sens.reshape(directions, fields, cells // tile, planes, tile)
    return new_state, new_sens.transpose(0, 1, 3, 2, 4).reshape(tangents.shape)


def solution(mesh):
    in_specs = (
        P(None, "sp", "grp"), P("grp", None, "sp", None), P("grp"),
        P(), P(), P(), P(), P(), P(),
    )
    out_specs = (P(None, "sp", "grp"), P("grp", None, "sp", None))
    return jax.shard_map(shards, mesh=mesh, in_specs=in_specs, out_specs=out_specs, check_vma=False)
```

```python
import functools
import math

import jax
import jax.numpy as jnp
from jax import lax
from jax.experimental import pallas as pl
from jax.experimental.pallas import tpu as pltpu
from jax.sharding import PartitionSpec as P

GRID_POINTS_THREE = 32
TIME_STEP = 0.2
ONE_LOW = 2.0**-10
MESH = pl.DeviceIdType.MESH
F32 = jnp.float32
BF16 = jnp.bfloat16


def in_plane(x, lane):
    cells = x.shape[1]
    width = GRID_POINTS_THREE
    before = jnp.where(
        lane == 0, pltpu.roll(x, cells - (width - 1), 1), pltpu.roll(x, 1, 1)
    )
    after = jnp.where(
        lane == width - 1, pltpu.roll(x, width - 1, 1), pltpu.roll(x, cells - 1, 1)
    )
    return before + after + (pltpu.roll(x, width, 1) + pltpu.roll(x, cells - width, 1))


def stacked(x, extra, species, row):
    base = species // 8 * 8
    tail = x[base:]
    tail = jnp.where(row == species + 1, 1.0 + ONE_LOW, jnp.where(row >= species, extra, tail))
    full = jnp.concatenate([x[:base], tail], 0)
    high = full.astype(BF16).astype(F32)
    return jnp.concatenate([high, full - high], 0).astype(BF16)


def halves(x):
    high = x.astype(BF16).astype(F32)
    return high, x - high


def with_heat(p, species, row):
    base = species // 8 * 8
    tail = p[base:]
    heat = p[species : species + 1] + p[species + 1 : species + 2]
    tail = jnp.where(row < species, tail, jnp.where(row == species, heat, 0.0))
    return jnp.concatenate([p[:base], tail], 0)


def column(vector, rows):
    count = vector.shape[0]
    wide = jnp.broadcast_to(vector.reshape(1, count), (rows, count))
    diagonal = lax.broadcasted_iota(jnp.int32, (rows, count), 0) == lax.broadcasted_iota(
        jnp.int32, (rows, count), 1
    )
    return jnp.sum(jnp.where(diagonal, wide, 0.0), axis=1, keepdims=True)


def build_weights(
    species, directions, react, product, lna, energy, diffus, enthalpy, index,
    w_nominal, w_tangent, w_net, spread, wide, flat,
):
    rows = w_net.shape[0]
    reactions = react.shape[1]
    depth = w_nominal.shape[0]
    nu_in = react[...].astype(F32)
    nu_net = (product[...] - react[...]).astype(F32)
    e_high, e_low = halves(energy[...].reshape(1, reactions))
    a_high, a_low = halves(lna[...].reshape(1, reactions))
    wide[...] = jnp.zeros_like(wide)
    for base, one in ((0, a_high), (rows, a_low * (1.0 / ONE_LOW))):
        wide[base : base + species, :reactions] = nu_in
        wide[base + species : base + species + 1, :reactions] = e_high
        wide[base + species + 1 : base + species + 2, :reactions] = one
        wide[base + species + 2 : base + species + 3, :reactions] = e_low
    nominal = jnp.transpose(wide[...])[:depth]
    w_nominal[...] = nominal.astype(BF16)
    reaction = lax.broadcasted_iota(jnp.int32, nominal.shape, 0)
    place = lax.broadcasted_iota(jnp.int32, nominal.shape, 1)
    cleared = jnp.where(
        (place == species + 1) | (place == rows + species + 1), 0.0, nominal
    )
    for d in range(directions):
        chosen = (reaction == index[d]) & (place == species + 1)
        w_tangent[d] = jnp.where(chosen, 1.0, cleared).astype(BF16)
    heat = -jnp.sum(nu_net * column(enthalpy[...], species), axis=0, keepdims=True)
    h_high, h_low = halves(heat)
    flat[...] = jnp.zeros_like(flat)
    flat[:species, :reactions] = nu_net
    flat[species : species + 1, :reactions] = h_high
    flat[species + 1 : species + 2, :reactions] = h_low
    w_net[...] = flat[...][:, :depth].astype(BF16)
    spread[...] = jnp.broadcast_to(column(diffus[...], rows), spread.shape)


def kernel(
    species, groups, ring,
    s_ref, t_ref, react_hbm, product_hbm, lna_hbm, energy_hbm, diffus_hbm, enthalpy_hbm, index,
    ns_ref, nt_ref,
    react, product, lna, energy, diffus, enthalpy,
    w_nominal, w_tangent, w_net, spread_ref, wide, flat,
    raw, st, zs, mid, rates, prods, inverses, tt, mt, part, ns_full,
    st_send, st_recv, near_send, near_recv, far_send, far_recv, local_sem,
):
    directions = t_ref.shape[0]
    rows, cells = w_net.shape[0], zs.shape[2]
    own_cells = s_ref.shape[2]
    fields = species + 1
    base = species // 8 * 8
    cuts = near_send.shape[0] // directions
    g = lax.axis_index("grp")
    i = lax.axis_index("sp")
    odd = lax.rem(i, 2)
    partner = i + 1 - 2 * odd
    ahead = lax.rem(i + 2 - 4 * odd + ring, ring)
    behind = lax.rem(i - 2 + 4 * odd + ring, ring)
    near_side, far_side = 2 * (1 - odd), 2 * odd
    near_k, far_k = 3 * (1 - odd), 3 * odd
    peers = [lax.rem(g + k, groups) for k in range(1, groups)]

    def remote(src, dst, send, recv, target):
        return pltpu.make_async_remote_copy(
            src_ref=src, dst_ref=dst, send_sem=send, recv_sem=recv,
            device_id=target, device_id_type=MESH,
        )

    locals_ = [
        pltpu.make_async_copy(src, dst, local_sem.at[n])
        for n, (src, dst) in enumerate(
            [
                (t_ref, raw.at[1]), (s_ref, st.at[1, g]), (react_hbm, react),
                (product_hbm, product), (lna_hbm, lna), (energy_hbm, energy),
                (diffus_hbm, diffus), (enthalpy_hbm, enthalpy),
            ]
        )
    ]
    for copy in locals_[2:]:
        copy.start()

    barrier = pltpu.get_barrier_semaphore()
    for target in [(g, partner), (g, ahead), (g, behind)] + [(p, i) for p in peers]:
        pl.semaphore_signal(barrier, inc=1, device_id=target, device_id_type=MESH)
    for copy in locals_[:2]:
        copy.start()
    pl.semaphore_wait(barrier, 3 + len(peers))

    s_near = remote(s_ref, st.at[2 * odd, g], st_send.at[0], st_recv.at[2 * odd, g], (g, partner))
    s_near_in = remote(s_ref, st.at[near_side, g], st_send.at[0], st_recv.at[near_side, g], (g, partner))
    s_far = remote(st.at[near_side, g], st.at[far_side, g], st_send.at[1], st_recv.at[far_side, g], (g, ahead))

    def to_group(src, side, first):
        return [
            remote(src, st.at[side, g], st_send.at[first + k], st_recv.at[side, g], (p, i))
            for k, p in enumerate(peers)
        ]

    def window(buffer, c):
        d, h = c // cuts, lax.rem(c, cuts)
        return buffer.at[d, pl.ds(h * (fields // cuts), fields // cuts)]

    def near(c):
        return remote(
            window(t_ref, c), window(raw.at[2 * odd], c), near_send.at[c], near_recv.at[c], (g, partner)
        )

    def far(c):
        return remote(
            window(raw.at[near_side], c), window(raw.at[far_side], c),
            far_send.at[c], far_recv.at[c], (g, ahead),
        )

    def unpack(side, d):
        block = raw[side, d]
        block = jnp.concatenate([block, jnp.zeros((rows - fields,) + block.shape[1:], F32)], 0)
        block = jnp.swapaxes(block, 0, 1)
        for q in range(block.shape[0]):
            lanes = block.shape[2]
            tt[2 * side + q % 2, d, :, q // 2 * lanes : (q // 2 + 1) * lanes] = block[q]

    pieces = cuts * directions

    def forward(c):
        near(c).wait_recv()
        far(c).start()

    def span(low, high, step):
        lax.fori_loop(low, high, lambda c, carry: (step(c), carry)[1], 0)

    s_near.start()
    group_own = to_group(s_ref, 1, 2)
    for copy in group_own:
        copy.start()
    span(0, pieces, lambda c: near(c).start())

    for copy in locals_[2:]:
        copy.wait()
    build_weights(
        species, directions, react, product, lna, energy, diffus, enthalpy, index,
        w_nominal, w_tangent, w_net, spread_ref, wide, flat,
    )
    row = lax.broadcasted_iota(jnp.int32, (rows - base, cells), 0) + base
    lane = lax.rem(
        lax.broadcasted_iota(jnp.int32, (rows, cells), 1), jnp.int32(GRID_POINTS_THREE)
    )

    def arrived(side):
        for p in peers:
            remote(
                st.at[side, p], st.at[side, p], st_send.at[0], st_recv.at[side, p], (p, i)
            ).wait_recv()
        for q in range(groups):
            slab = st[side, q]
            slab = jnp.concatenate([slab, jnp.zeros((rows - fields,) + slab.shape[1:], F32)], 0)
            slab = jnp.swapaxes(slab, 0, 1)
            for p in range(2):
                zs[2 * side + p, :, q * own_cells : (q + 1) * own_cells] = slab[p]

    def nominal(z, slot):
        level = 1.0 / z[species : species + 1]
        rate = jnp.exp(
            jnp.dot(
                w_nominal[...], stacked(z, -level, species, row), preferred_element_type=F32
            )
        )
        rates[slot] = rate
        high, low = halves(rate)
        production = jnp.dot(
            w_net[...], high.astype(BF16), preferred_element_type=F32
        ) + jnp.dot(w_net[...], low.astype(BF16), preferred_element_type=F32)
        inverse = jnp.exp(-z)
        inverse = jnp.concatenate([inverse[:base], jnp.where(row < species, inverse[base:], 1.0)], 0)
        inverses[slot] = inverse
        prods[slot] = jnp.concatenate(
            [production[:base], jnp.where(row < species, production[base:], 0.0)], 0
        )
        return with_heat(production, species, row) * inverse

    def tangent(u, z, slot, d):
        level = 1.0 / z[species : species + 1]
        change = jnp.dot(
            w_tangent[d],
            stacked(u, u[species : species + 1] * (level * level), species, row),
            preferred_element_type=F32,
        )
        moved = jnp.dot(
            w_net[...], (rates[slot] * change).astype(BF16), preferred_element_type=F32
        )
        return (with_heat(moved, species, row) - prods[slot] * u) * inverses[slot]

    def lap(low, x, high):
        return low + high + in_plane(x, lane) - 6.0 * x

    s_near_in.wait_recv()
    s_far.start()
    group_near = to_group(st.at[near_side, g], near_side, 2 + len(peers))
    for copy in group_near:
        copy.start()
    locals_[1].wait()
    arrived(1)
    for k in (1, 2):
        mid[k] = nominal(zs[k + 1], k)
    locals_[0].wait()
    span(0, cuts // 2, forward)
    s_far.wait_recv()
    group_far = to_group(st.at[far_side, g], far_side, 2 + 2 * len(peers))
    for copy in group_far:
        copy.start()
    span(cuts // 2, cuts, forward)

    def own_planes(d, carry):
        spread = spread_ref[...]
        unpack(1, d)
        for k in (1, 2):
            u = tt[k + 1, d]
            inner = tt[4 - k, d] + in_plane(u, lane) - 6.0 * u
            part[d, k - 1] = tangent(u, zs[k + 1], k, d) + spread * inner
        forward(cuts + d)
        return carry

    lax.fori_loop(0, directions, own_planes, 0)
    done = cuts + directions

    arrived(near_side)
    mid[near_k] = nominal(zs[near_k + 1], near_k)
    span(done, done + 1, forward)
    arrived(far_side)
    mid[far_k] = nominal(zs[far_k + 1], far_k)
    for k in range(4):
        z = zs[k + 1]
        rate = mid[k] + spread_ref[...] * lap(zs[k], z, zs[k + 2])
        mid[k] = z + TIME_STEP * rate
        if k in (1, 2):
            ns_full[k - 1] = z + 0.5 * TIME_STEP * rate
    span(done + 1, done + 2, forward)
    for k in (1, 2):
        z = mid[k]
        rate = nominal(z, k + 3) + spread_ref[...] * lap(mid[k - 1], z, mid[k + 1])
        ns_full[k - 1] += 0.5 * TIME_STEP * rate
    own = pl.ds(pl.multiple_of(g * own_cells, own_cells), own_cells)
    ns_ref[...] = jnp.swapaxes(ns_full[:, :, own], 0, 1)[:fields]
    span(done + 2, cuts * (directions - 1), forward)

    def halo(k, d):
        u = tt[k + 1, d]
        rate = tangent(u, zs[k + 1], k, d) + spread_ref[...] * lap(tt[k, d], u, tt[k + 2, d])
        mt[k] = u + TIME_STEP * rate

    def direction(d, carry):
        @pl.when(d == directions - 2)
        def _():
            span(cuts * (directions - 1), pieces, forward)

        unpack(near_side, d)
        halo(near_k, d)
        span(cuts * d, cuts * d + cuts, lambda c: far(c).wait_recv())
        unpack(far_side, d)
        spread = spread_ref[...]
        halo(far_k, d)
        for k in (1, 2):
            u = tt[k + 1, d]
            rate = part[d, k - 1] + spread * tt[3 * k - 2, d]
            mt[k] = u + TIME_STEP * rate
            part[d, k - 1] = u + 0.5 * TIME_STEP * rate
        for k in (1, 2):
            u = mt[k]
            rate = tangent(u, mid[k], k + 3, d) + spread * lap(mt[k - 1], u, mt[k + 1])
            part[d, k - 1] += 0.5 * TIME_STEP * rate
        lanes = t_ref.shape[3]
        tiles = [
            part[d, p, :, q * lanes : (q + 1) * lanes] for q in range(cells // lanes) for p in range(2)
        ]
        nt_ref[d] = jnp.swapaxes(jnp.stack(tiles, 0), 0, 1)[:fields]
        return carry

    lax.fori_loop(0, directions, direction, 0)

    s_near.wait_send()
    s_far.wait_send()
    for copy in group_own + group_near + group_far:
        copy.wait_send()

    def sent(c):
        near(c).wait_send()
        far(c).wait_send()

    span(0, pieces, sent)


def shards(
    flame_state, tangents, direction_index, reactant_table, product_table,
    natural_log_frequency, arrhenius_energy, diffusivity, enthalpy,
):
    fields, planes, own_cells = flame_state.shape
    directions, cells = tangents.shape[0], tangents.shape[3]
    reactions, species = reactant_table.shape
    groups, ring = lax.axis_size("grp"), lax.axis_size("sp")
    assert planes == 2 and ring % 2 == 0 and directions >= 3
    rows = -(-(species + 3) // 8) * 8
    assert species % 8 <= 5
    depth = -(-reactions // 16) * 16
    lanes = -(-reactions // 128) * 128
    tile = math.gcd(cells, 128)

    sens = tangents.reshape(directions, fields, planes, cells // tile, tile).transpose(0, 1, 3, 2, 4)
    sens = sens.reshape(directions, fields, planes * cells // tile, tile)

    vmem = pl.BlockSpec(memory_space=pltpu.VMEM)
    anywhere = pl.BlockSpec(memory_space=pl.ANY)
    hbm = pl.BlockSpec(memory_space=pltpu.HBM)
    smem = pl.BlockSpec(memory_space=pltpu.SMEM)
    pieces = math.gcd(fields, 6) * directions
    new_state, new_sens = pl.pallas_call(
        functools.partial(kernel, species, groups, ring),
        out_shape=(
            jax.ShapeDtypeStruct(flame_state.shape, F32),
            jax.ShapeDtypeStruct(sens.shape, F32),
        ),
        in_specs=[anywhere, anywhere] + [hbm] * 6 + [smem],
        out_specs=(vmem, vmem),
        scratch_shapes=[
            pltpu.VMEM((species, reactions), jnp.int32),
            pltpu.VMEM((species, reactions), jnp.int32),
            pltpu.VMEM((reactions,), F32),
            pltpu.VMEM((reactions,), F32),
            pltpu.VMEM((fields,), F32),
            pltpu.VMEM((species,), F32),
            pltpu.VMEM((depth, 2 * rows), BF16),
            pltpu.VMEM((directions, depth, 2 * rows), BF16),
            pltpu.VMEM((rows, depth), BF16),
            pltpu.VMEM((rows, cells), F32),
            pltpu.VMEM((2 * rows, lanes), F32),
            pltpu.VMEM((rows, lanes), F32),
            pltpu.VMEM((3,) + sens.shape, F32),
            pltpu.VMEM((3, groups) + flame_state.shape, F32),
            pltpu.VMEM((6, rows, cells), F32),
            pltpu.VMEM((4, rows, cells), F32),
            pltpu.VMEM((6, depth, cells), F32),
            pltpu.VMEM((6, rows, cells), F32),
            pltpu.VMEM((6, rows, cells), F32),
            pltpu.VMEM((6, directions, rows, cells), F32),
            pltpu.VMEM((4, rows, cells), F32),
            pltpu.VMEM((directions, 2, rows, cells), F32),
            pltpu.VMEM((2, rows, cells), F32),
            pltpu.SemaphoreType.DMA((2 + 3 * (groups - 1),)),
            pltpu.SemaphoreType.DMA((3, groups)),
            pltpu.SemaphoreType.DMA((pieces,)),
            pltpu.SemaphoreType.DMA((pieces,)),
            pltpu.SemaphoreType.DMA((pieces,)),
            pltpu.SemaphoreType.DMA((pieces,)),
            pltpu.SemaphoreType.DMA((8,)),
        ],
        compiler_params=pltpu.CompilerParams(
            collective_id=0, has_side_effects=True, vmem_limit_bytes=67043328

        ),
        name="step",
    )(
        flame_state, sens, reactant_table.T, product_table.T, natural_log_frequency,
        arrhenius_energy, diffusivity, enthalpy, direction_index,
    )
    new_sens = new_sens.reshape(directions, fields, cells // tile, planes, tile)
    return new_state, new_sens.transpose(0, 1, 3, 2, 4).reshape(tangents.shape)


def solution(mesh):
    in_specs = (
        P(None, "sp", "grp"), P("grp", None, "sp", None), P("grp"),
        P(), P(), P(), P(), P(), P(),
    )
    out_specs = (P(None, "sp", "grp"), P("grp", None, "sp", None))
    return jax.shard_map(shards, mesh=mesh, in_specs=in_specs, out_specs=out_specs, check_vma=False)
```

```python
import functools
import math

import jax
import jax.numpy as jnp
from jax import lax
from jax.experimental import pallas as pl
from jax.experimental.pallas import tpu as pltpu
from jax.sharding import PartitionSpec as P

GRID_POINTS_THREE = 32
TIME_STEP = 0.2
ONE_LOW = 2.0**-10
MESH = pl.DeviceIdType.MESH
F32 = jnp.float32
BF16 = jnp.bfloat16


def in_plane(x, lane):
    cells = x.shape[1]
    width = GRID_POINTS_THREE
    before = jnp.where(
        lane == 0, pltpu.roll(x, cells - (width - 1), 1), pltpu.roll(x, 1, 1)
    )
    after = jnp.where(
        lane == width - 1, pltpu.roll(x, width - 1, 1), pltpu.roll(x, cells - 1, 1)
    )
    return before + after + (pltpu.roll(x, width, 1) + pltpu.roll(x, cells - width, 1))


def stacked(x, extra, species, row):
    base = species // 8 * 8
    tail = x[base:]
    tail = jnp.where(row == species + 1, 1.0 + ONE_LOW, jnp.where(row >= species, extra, tail))
    full = jnp.concatenate([x[:base], tail], 0)
    high = full.astype(BF16).astype(F32)
    return jnp.concatenate([high, full - high], 0).astype(BF16)


def halves(x):
    high = x.astype(BF16).astype(F32)
    return high, x - high


def with_heat(p, species, row):
    base = species // 8 * 8
    tail = p[base:]
    heat = p[species : species + 1] + p[species + 1 : species + 2]
    tail = jnp.where(row < species, tail, jnp.where(row == species, heat, 0.0))
    return jnp.concatenate([p[:base], tail], 0)


def column(vector, rows):
    count = vector.shape[0]
    wide = jnp.broadcast_to(vector.reshape(1, count), (rows, count))
    diagonal = lax.broadcasted_iota(jnp.int32, (rows, count), 0) == lax.broadcasted_iota(
        jnp.int32, (rows, count), 1
    )
    return jnp.sum(jnp.where(diagonal, wide, 0.0), axis=1, keepdims=True)


def build_weights(
    species, directions, react, product, lna, energy, diffus, enthalpy, index,
    w_nominal, w_tangent, w_net, spread, wide, flat,
):
    rows = w_net.shape[0]
    reactions = react.shape[1]
    depth = w_nominal.shape[0]
    nu_in = react[...].astype(F32)
    nu_net = (product[...] - react[...]).astype(F32)
    e_high, e_low = halves(energy[...].reshape(1, reactions))
    a_high, a_low = halves(lna[...].reshape(1, reactions))
    wide[...] = jnp.zeros_like(wide)
    for base, one in ((0, a_high), (rows, a_low * (1.0 / ONE_LOW))):
        wide[base : base + species, :reactions] = nu_in
        wide[base + species : base + species + 1, :reactions] = e_high
        wide[base + species + 1 : base + species + 2, :reactions] = one
        wide[base + species + 2 : base + species + 3, :reactions] = e_low
    nominal = jnp.transpose(wide[...])[:depth]
    w_nominal[...] = nominal.astype(BF16)
    reaction = lax.broadcasted_iota(jnp.int32, nominal.shape, 0)
    place = lax.broadcasted_iota(jnp.int32, nominal.shape, 1)
    cleared = jnp.where(
        (place == species + 1) | (place == rows + species + 1), 0.0, nominal
    )
    for d in range(directions):
        chosen = (reaction == index[d]) & (place == species + 1)
        w_tangent[d] = jnp.where(chosen, 1.0, cleared).astype(BF16)
    heat = -jnp.sum(nu_net * column(enthalpy[...], species), axis=0, keepdims=True)
    h_high, h_low = halves(heat)
    flat[...] = jnp.zeros_like(flat)
    flat[:species, :reactions] = nu_net
    flat[species : species + 1, :reactions] = h_high
    flat[species + 1 : species + 2, :reactions] = h_low
    w_net[...] = flat[...][:, :depth].astype(BF16)
    spread[...] = jnp.broadcast_to(column(diffus[...], rows), spread.shape)


def kernel(
    species, groups, ring,
    s_ref, t_ref, react_hbm, product_hbm, lna_hbm, energy_hbm, diffus_hbm, enthalpy_hbm, index_hbm,
    ns_ref, nt_ref, index,
    react, product, lna, energy, diffus, enthalpy,
    w_nominal, w_tangent, w_net, spread_ref, wide, flat,
    raw, st, zs, mid, rates, prods, inverses, tt, mt, part, ns_full,
    st_send, st_recv, near_send, near_recv, far_send, far_recv, local_sem,
):
    directions = t_ref.shape[0]
    rows, cells = w_net.shape[0], zs.shape[2]
    own_cells = s_ref.shape[2]
    fields = species + 1
    base = species // 8 * 8
    cuts = near_send.shape[0] // directions
    g = lax.axis_index("grp")
    i = lax.axis_index("sp")
    odd = lax.rem(i, 2)
    partner = i + 1 - 2 * odd
    ahead = lax.rem(i + 2 - 4 * odd + ring, ring)
    behind = lax.rem(i - 2 + 4 * odd + ring, ring)
    near_side, far_side = 2 * (1 - odd), 2 * odd
    near_k, far_k = 3 * (1 - odd), 3 * odd
    peers = [lax.rem(g + k, groups) for k in range(1, groups)]

    def remote(src, dst, send, recv, target):
        return pltpu.make_async_remote_copy(
            src_ref=src, dst_ref=dst, send_sem=send, recv_sem=recv,
            device_id=target, device_id_type=MESH,
        )

    locals_ = [
        pltpu.make_async_copy(src, dst, local_sem.at[n])
        for n, (src, dst) in enumerate(
            [
                (t_ref, raw.at[1]), (s_ref, st.at[1, g]), (react_hbm, react),
                (product_hbm, product), (lna_hbm, lna), (energy_hbm, energy),
                (diffus_hbm, diffus), (enthalpy_hbm, enthalpy),
                (index_hbm, index),
            ]
        )
    ]
    for copy in locals_[2:]:
        copy.start()

    barrier = pltpu.get_barrier_semaphore()
    for target in [(g, partner), (g, ahead), (g, behind)] + [(p, i) for p in peers]:
        pl.semaphore_signal(barrier, inc=1, device_id=target, device_id_type=MESH)
    for copy in locals_[:2]:
        copy.start()
    pl.semaphore_wait(barrier, 3 + len(peers))

    s_near = remote(s_ref, st.at[2 * odd, g], st_send.at[0], st_recv.at[2 * odd, g], (g, partner))
    s_near_in = remote(s_ref, st.at[near_side, g], st_send.at[0], st_recv.at[near_side, g], (g, partner))
    s_far = remote(st.at[near_side, g], st.at[far_side, g], st_send.at[1], st_recv.at[far_side, g], (g, ahead))

    def to_group(src, side, first):
        return [
            remote(src, st.at[side, g], st_send.at[first + k], st_recv.at[side, g], (p, i))
            for k, p in enumerate(peers)
        ]

    def window(buffer, c):
        d, h = c // cuts, lax.rem(c, cuts)
        return buffer.at[d, pl.ds(h * (fields // cuts), fields // cuts)]

    def near(c):
        return remote(
            window(t_ref, c), window(raw.at[2 * odd], c), near_send.at[c], near_recv.at[c], (g, partner)
        )

    def far(c):
        return remote(
            window(raw.at[near_side], c), window(raw.at[far_side], c),
            far_send.at[c], far_recv.at[c], (g, ahead),
        )

    def unpack(side, d):
        block = raw[side, d]
        block = jnp.concatenate([block, jnp.zeros((rows - fields,) + block.shape[1:], F32)], 0)
        block = jnp.swapaxes(block, 0, 1)
        for q in range(block.shape[0]):
            lanes = block.shape[2]
            tt[2 * side + q % 2, d, :, q // 2 * lanes : (q // 2 + 1) * lanes] = block[q]

    pieces = cuts * directions

    def forward(c):
        near(c).wait_recv()
        far(c).start()

    def span(low, high, step):
        lax.fori_loop(low, high, lambda c, carry: (step(c), carry)[1], 0)

    s_near.start()
    group_own = to_group(s_ref, 1, 2)
    for copy in group_own:
        copy.start()
    span(0, pieces, lambda c: near(c).start())

    for copy in locals_[2:]:
        copy.wait()
    build_weights(
        species, directions, react, product, lna, energy, diffus, enthalpy, index,
        w_nominal, w_tangent, w_net, spread_ref, wide, flat,
    )
    row = lax.broadcasted_iota(jnp.int32, (rows - base, cells), 0) + base
    lane = lax.rem(
        lax.broadcasted_iota(jnp.int32, (rows, cells), 1), jnp.int32(GRID_POINTS_THREE)
    )

    def arrived(side):
        for p in peers:
            remote(
                st.at[side, p], st.at[side, p], st_send.at[0], st_recv.at[side, p], (p, i)
            ).wait_recv()
        for q in range(groups):
            slab = st[side, q]
            slab = jnp.concatenate([slab, jnp.zeros((rows - fields,) + slab.shape[1:], F32)], 0)
            slab = jnp.swapaxes(slab, 0, 1)
            for p in range(2):
                zs[2 * side + p, :, q * own_cells : (q + 1) * own_cells] = slab[p]

    def nominal(z, slot):
        level = 1.0 / z[species : species + 1]
        rate = jnp.exp(
            jnp.dot(
                w_nominal[...], stacked(z, -level, species, row), preferred_element_type=F32
            )
        )
        rates[slot] = rate
        high, low = halves(rate)
        production = jnp.dot(
            w_net[...], high.astype(BF16), preferred_element_type=F32
        ) + jnp.dot(w_net[...], low.astype(BF16), preferred_element_type=F32)
        inverse = jnp.exp(-z)
        inverse = jnp.concatenate([inverse[:base], jnp.where(row < species, inverse[base:], 1.0)], 0)
        inverses[slot] = inverse
        prods[slot] = jnp.concatenate(
            [production[:base], jnp.where(row < species, production[base:], 0.0)], 0
        )
        return with_heat(production, species, row) * inverse

    def tangent(u, z, slot, d):
        level = 1.0 / z[species : species + 1]
        change = jnp.dot(
            w_tangent[d],
            stacked(u, u[species : species + 1] * (level * level), species, row),
            preferred_element_type=F32,
        )
        moved = jnp.dot(
            w_net[...], (rates[slot] * change).astype(BF16), preferred_element_type=F32
        )
        return (with_heat(moved, species, row) - prods[slot] * u) * inverses[slot]

    def lap(low, x, high):
        return low + high + in_plane(x, lane) - 6.0 * x

    s_near_in.wait_recv()
    s_far.start()
    group_near = to_group(st.at[near_side, g], near_side, 2 + len(peers))
    for copy in group_near:
        copy.start()
    locals_[1].wait()
    arrived(1)
    for k in (1, 2):
        mid[k] = nominal(zs[k + 1], k)
    locals_[0].wait()
    span(0, cuts // 2, forward)
    s_far.wait_recv()
    group_far = to_group(st.at[far_side, g], far_side, 2 + 2 * len(peers))
    for copy in group_far:
        copy.start()
    span(cuts // 2, cuts, forward)

    def own_planes(d, carry):
        spread = spread_ref[...]
        unpack(1, d)
        for k in (1, 2):
            u = tt[k + 1, d]
            inner = tt[4 - k, d] + in_plane(u, lane) - 6.0 * u
            part[d, k - 1] = tangent(u, zs[k + 1], k, d) + spread * inner
        forward(cuts + d)
        return carry

    lax.fori_loop(0, directions, own_planes, 0)
    done = cuts + directions

    arrived(near_side)
    mid[near_k] = nominal(zs[near_k + 1], near_k)
    span(done, done + 1, forward)
    arrived(far_side)
    mid[far_k] = nominal(zs[far_k + 1], far_k)
    for k in range(4):
        z = zs[k + 1]
        rate = mid[k] + spread_ref[...] * lap(zs[k], z, zs[k + 2])
        mid[k] = z + TIME_STEP * rate
        if k in (1, 2):
            ns_full[k - 1] = z + 0.5 * TIME_STEP * rate
    span(done + 1, done + 2, forward)
    for k in (1, 2):
        z = mid[k]
        rate = nominal(z, k + 3) + spread_ref[...] * lap(mid[k - 1], z, mid[k + 1])
        ns_full[k - 1] += 0.5 * TIME_STEP * rate
    own = pl.ds(pl.multiple_of(g * own_cells, own_cells), own_cells)
    ns_ref[...] = jnp.swapaxes(ns_full[:, :, own], 0, 1)[:fields]
    span(done + 2, cuts * (directions - 1), forward)

    def halo(k, d):
        u = tt[k + 1, d]
        rate = tangent(u, zs[k + 1], k, d) + spread_ref[...] * lap(tt[k, d], u, tt[k + 2, d])
        mt[k] = u + TIME_STEP * rate

    def direction(d, carry):
        @pl.when(d == directions - 2)
        def _():
            span(cuts * (directions - 1), pieces, forward)

        unpack(near_side, d)
        halo(near_k, d)
        span(cuts * d, cuts * d + cuts, lambda c: far(c).wait_recv())
        unpack(far_side, d)
        spread = spread_ref[...]
        halo(far_k, d)
        for k in (1, 2):
            u = tt[k + 1, d]
            rate = part[d, k - 1] + spread * tt[3 * k - 2, d]
            mt[k] = u + TIME_STEP * rate
            part[d, k - 1] = u + 0.5 * TIME_STEP * rate
        for k in (1, 2):
            u = mt[k]
            rate = tangent(u, mid[k], k + 3, d) + spread * lap(mt[k - 1], u, mt[k + 1])
            part[d, k - 1] += 0.5 * TIME_STEP * rate
        lanes = t_ref.shape[3]
        tiles = [
            part[d, p, :, q * lanes : (q + 1) * lanes] for q in range(cells // lanes) for p in range(2)
        ]
        nt_ref[d] = jnp.swapaxes(jnp.stack(tiles, 0), 0, 1)[:fields]
        return carry

    lax.fori_loop(0, directions, direction, 0)

    s_near.wait_send()
    s_far.wait_send()
    for copy in group_own + group_near + group_far:
        copy.wait_send()

    def sent(c):
        near(c).wait_send()
        far(c).wait_send()

    span(0, pieces, sent)


def shards(
    flame_state, tangents, direction_index, reactant_table, product_table,
    natural_log_frequency, arrhenius_energy, diffusivity, enthalpy,
):
    fields, planes, own_cells = flame_state.shape
    directions, cells = tangents.shape[0], tangents.shape[3]
    reactions, species = reactant_table.shape
    groups, ring = lax.axis_size("grp"), lax.axis_size("sp")
    assert planes == 2 and ring % 2 == 0 and directions >= 3
    rows = -(-(species + 3) // 8) * 8
    assert species % 8 <= 5
    depth = -(-reactions // 16) * 16
    lanes = -(-reactions // 128) * 128
    tile = math.gcd(cells, 128)

    sens = tangents.reshape(directions, fields, planes, cells // tile, tile).transpose(0, 1, 3, 2, 4)
    sens = sens.reshape(directions, fields, planes * cells // tile, tile)

    vmem = pl.BlockSpec(memory_space=pltpu.VMEM)
    anywhere = pl.BlockSpec(memory_space=pl.ANY)
    hbm = pl.BlockSpec(memory_space=pltpu.HBM)
    pieces = math.gcd(fields, 6) * directions
    new_state, new_sens = pl.pallas_call(
        functools.partial(kernel, species, groups, ring),
        out_shape=(
            jax.ShapeDtypeStruct(flame_state.shape, F32),
            jax.ShapeDtypeStruct(sens.shape, F32),
        ),
        in_specs=[anywhere, anywhere] + [hbm] * 7,
        out_specs=(vmem, vmem),
        scratch_shapes=[
            pltpu.SMEM((directions,), jnp.int32),
            pltpu.VMEM((species, reactions), jnp.int32),
            pltpu.VMEM((species, reactions), jnp.int32),
            pltpu.VMEM((reactions,), F32),
            pltpu.VMEM((reactions,), F32),
            pltpu.VMEM((fields,), F32),
            pltpu.VMEM((species,), F32),
            pltpu.VMEM((depth, 2 * rows), BF16),
            pltpu.VMEM((directions, depth, 2 * rows), BF16),
            pltpu.VMEM((rows, depth), BF16),
            pltpu.VMEM((rows, cells), F32),
            pltpu.VMEM((2 * rows, lanes), F32),
            pltpu.VMEM((rows, lanes), F32),
            pltpu.VMEM((3,) + sens.shape, F32),
            pltpu.VMEM((3, groups) + flame_state.shape, F32),
            pltpu.VMEM((6, rows, cells), F32),
            pltpu.VMEM((4, rows, cells), F32),
            pltpu.VMEM((6, depth, cells), F32),
            pltpu.VMEM((6, rows, cells), F32),
            pltpu.VMEM((6, rows, cells), F32),
            pltpu.VMEM((6, directions, rows, cells), F32),
            pltpu.VMEM((4, rows, cells), F32),
            pltpu.VMEM((directions, 2, rows, cells), F32),
            pltpu.VMEM((2, rows, cells), F32),
            pltpu.SemaphoreType.DMA((2 + 3 * (groups - 1),)),
            pltpu.SemaphoreType.DMA((3, groups)),
            pltpu.SemaphoreType.DMA((pieces,)),
            pltpu.SemaphoreType.DMA((pieces,)),
            pltpu.SemaphoreType.DMA((pieces,)),
            pltpu.SemaphoreType.DMA((pieces,)),
            pltpu.SemaphoreType.DMA((9,)),
        ],
        compiler_params=pltpu.CompilerParams(
            collective_id=0, has_side_effects=True, vmem_limit_bytes=48 << 20
        ),
        name="step",
    )(
        *[
            pltpu.with_memory_space_constraint(x, pltpu.HBM)
            for x in (
                flame_state, sens, reactant_table.T, product_table.T, natural_log_frequency,
                arrhenius_energy, diffusivity, enthalpy, direction_index,
            )
        ],
    )
    new_sens = new_sens.reshape(directions, fields, cells // tile, planes, tile)
    return new_state, new_sens.transpose(0, 1, 3, 2, 4).reshape(tangents.shape)


def solution(mesh):
    in_specs = (
        P(None, "sp", "grp"), P("grp", None, "sp", None), P("grp"),
        P(), P(), P(), P(), P(), P(),
    )
    out_specs = (P(None, "sp", "grp"), P("grp", None, "sp", None))
    return jax.shard_map(shards, mesh=mesh, in_specs=in_specs, out_specs=out_specs, check_vma=False)
```

```python
import functools
import math

import jax
import jax.numpy as jnp
from jax import lax
from jax.experimental import pallas as pl
from jax.experimental.pallas import tpu as pltpu
from jax.sharding import PartitionSpec as P

GRID_POINTS_THREE = 32
TIME_STEP = 0.2
ONE_LOW = 2.0**-10
MESH = pl.DeviceIdType.MESH
F32 = jnp.float32
BF16 = jnp.bfloat16


def in_plane(x, lane):
    cells = x.shape[1]
    width = GRID_POINTS_THREE
    before = jnp.where(
        lane == 0, pltpu.roll(x, cells - (width - 1), 1), pltpu.roll(x, 1, 1)
    )
    after = jnp.where(
        lane == width - 1, pltpu.roll(x, width - 1, 1), pltpu.roll(x, cells - 1, 1)
    )
    return before + after + (pltpu.roll(x, width, 1) + pltpu.roll(x, cells - width, 1))


def stacked(x, extra, species, row):
    base = species // 8 * 8
    tail = x[base:]
    tail = jnp.where(row == species + 1, 1.0 + ONE_LOW, jnp.where(row >= species, extra, tail))
    full = jnp.concatenate([x[:base], tail], 0)
    high = full.astype(BF16).astype(F32)
    return jnp.concatenate([high, full - high], 0).astype(BF16)


def halves(x):
    high = x.astype(BF16).astype(F32)
    return high, x - high


def with_heat(p, species, row):
    base = species // 8 * 8
    tail = p[base:]
    heat = p[species : species + 1] + p[species + 1 : species + 2]
    tail = jnp.where(row < species, tail, jnp.where(row == species, heat, 0.0))
    return jnp.concatenate([p[:base], tail], 0)


def column(vector, rows):
    count = vector.shape[0]
    wide = jnp.broadcast_to(vector.reshape(1, count), (rows, count))
    diagonal = lax.broadcasted_iota(jnp.int32, (rows, count), 0) == lax.broadcasted_iota(
        jnp.int32, (rows, count), 1
    )
    return jnp.sum(jnp.where(diagonal, wide, 0.0), axis=1, keepdims=True)


def build_weights(
    species, directions, react, product, lna, energy, diffus, enthalpy, index,
    w_nominal, w_tangent, w_net, spread, wide, flat,
):
    rows = w_net.shape[0]
    reactions = react.shape[1]
    depth = w_nominal.shape[0]
    nu_in = react[...].astype(F32)
    nu_net = (product[...] - react[...]).astype(F32)
    e_high, e_low = halves(energy[...].reshape(1, reactions))
    a_high, a_low = halves(lna[...].reshape(1, reactions))
    wide[...] = jnp.zeros_like(wide)
    for base, one in ((0, a_high), (rows, a_low * (1.0 / ONE_LOW))):
        wide[base : base + species, :reactions] = nu_in
        wide[base + species : base + species + 1, :reactions] = e_high
        wide[base + species + 1 : base + species + 2, :reactions] = one
        wide[base + species + 2 : base + species + 3, :reactions] = e_low
    nominal = jnp.transpose(wide[...])[:depth]
    w_nominal[...] = nominal.astype(BF16)
    reaction = lax.broadcasted_iota(jnp.int32, nominal.shape, 0)
    place = lax.broadcasted_iota(jnp.int32, nominal.shape, 1)
    cleared = jnp.where(
        (place == species + 1) | (place == rows + species + 1), 0.0, nominal
    )
    for d in range(directions):
        chosen = (reaction == index[d]) & (place == species + 1)
        w_tangent[d] = jnp.where(chosen, 1.0, cleared).astype(BF16)
    heat = -jnp.sum(nu_net * column(enthalpy[...], species), axis=0, keepdims=True)
    h_high, h_low = halves(heat)
    flat[...] = jnp.zeros_like(flat)
    flat[:species, :reactions] = nu_net
    flat[species : species + 1, :reactions] = h_high
    flat[species + 1 : species + 2, :reactions] = h_low
    w_net[...] = flat[...][:, :depth].astype(BF16)
    spread[...] = jnp.broadcast_to(column(diffus[...], rows), spread.shape)


def kernel(
    species, groups, ring,
    s_ref, t_ref, react_hbm, product_hbm, lna_hbm, energy_hbm, diffus_hbm, enthalpy_hbm, index_hbm,
    ns_ref, nt_ref, index,
    react, product, lna, energy, diffus, enthalpy,
    w_nominal, w_tangent, w_net, spread_ref, wide, flat,
    raw, st, zs, mid, rates, prods, inverses, tt, mt, part, ns_full,
    st_send, st_recv, near_send, near_recv, far_send, far_recv, local_sem,
):
    directions = t_ref.shape[0]
    rows, cells = w_net.shape[0], zs.shape[2]
    own_cells = s_ref.shape[2]
    fields = species + 1
    base = species // 8 * 8
    cuts = near_send.shape[0] // directions
    g = lax.axis_index("grp")
    i = lax.axis_index("sp")
    odd = lax.rem(i, 2)
    partner = i + 1 - 2 * odd
    ahead = lax.rem(i + 2 - 4 * odd + ring, ring)
    behind = lax.rem(i - 2 + 4 * odd + ring, ring)
    near_side, far_side = 2 * (1 - odd), 2 * odd
    near_k, far_k = 3 * (1 - odd), 3 * odd
    peers = [lax.rem(g + k, groups) for k in range(1, groups)]

    def remote(src, dst, send, recv, target):
        return pltpu.make_async_remote_copy(
            src_ref=src, dst_ref=dst, send_sem=send, recv_sem=recv,
            device_id=target, device_id_type=MESH,
        )

    locals_ = [
        pltpu.make_async_copy(src, dst, local_sem.at[n])
        for n, (src, dst) in enumerate(
            [
                (t_ref, raw.at[1]), (s_ref, st.at[1, g]), (react_hbm, react),
                (product_hbm, product), (lna_hbm, lna), (energy_hbm, energy),
                (diffus_hbm, diffus), (enthalpy_hbm, enthalpy),
                (index_hbm, index),
            ]
        )
    ]
    for copy in locals_[2:]:
        copy.start()

    barrier = pltpu.get_barrier_semaphore()
    for target in [(g, partner), (g, ahead), (g, behind)] + [(p, i) for p in peers]:
        pl.semaphore_signal(barrier, inc=1, device_id=target, device_id_type=MESH)
    for copy in locals_[:2]:
        copy.start()
    pl.semaphore_wait(barrier, 3 + len(peers))

    s_near = remote(s_ref, st.at[2 * odd, g], st_send.at[0], st_recv.at[2 * odd, g], (g, partner))
    s_near_in = remote(s_ref, st.at[near_side, g], st_send.at[0], st_recv.at[near_side, g], (g, partner))
    s_far = remote(st.at[near_side, g], st.at[far_side, g], st_send.at[1], st_recv.at[far_side, g], (g, ahead))

    def to_group(src, side, first):
        return [
            remote(src, st.at[side, g], st_send.at[first + k], st_recv.at[side, g], (p, i))
            for k, p in enumerate(peers)
        ]

    def window(buffer, c):
        d, h = c // cuts, lax.rem(c, cuts)
        return buffer.at[d, pl.ds(h * (fields // cuts), fields // cuts)]

    def near(c):
        return remote(
            window(t_ref, c), window(raw.at[2 * odd], c), near_send.at[c], near_recv.at[c], (g, partner)
        )

    def far(c):
        return remote(
            window(raw.at[near_side], c), window(raw.at[far_side], c),
            far_send.at[c], far_recv.at[c], (g, ahead),
        )

    def unpack(side, d):
        block = raw[side, d]
        block = jnp.concatenate([block, jnp.zeros((rows - fields,) + block.shape[1:], F32)], 0)
        block = jnp.swapaxes(block, 0, 1)
        for q in range(block.shape[0]):
            lanes = block.shape[2]
            tt[2 * side + q % 2, d, :, q // 2 * lanes : (q // 2 + 1) * lanes] = block[q]

    pieces = cuts * directions

    def forward(c):
        near(c).wait_recv()
        far(c).start()

    def span(low, high, step):
        lax.fori_loop(low, high, lambda c, carry: (step(c), carry)[1], 0)

    s_near.start()
    group_own = to_group(s_ref, 1, 2)
    for copy in group_own:
        copy.start()
    span(0, pieces, lambda c: near(c).start())

    for copy in locals_[2:]:
        copy.wait()
    build_weights(
        species, directions, react, product, lna, energy, diffus, enthalpy, index,
        w_nominal, w_tangent, w_net, spread_ref, wide, flat,
    )
    row = lax.broadcasted_iota(jnp.int32, (rows - base, cells), 0) + base
    lane = lax.rem(
        lax.broadcasted_iota(jnp.int32, (rows, cells), 1), jnp.int32(GRID_POINTS_THREE)
    )

    def arrived(side):
        for p in peers:
            remote(
                st.at[side, p], st.at[side, p], st_send.at[0], st_recv.at[side, p], (p, i)
            ).wait_recv()
        for q in range(groups):
            slab = st[side, q]
            slab = jnp.concatenate([slab, jnp.zeros((rows - fields,) + slab.shape[1:], F32)], 0)
            slab = jnp.swapaxes(slab, 0, 1)
            for p in range(2):
                zs[2 * side + p, :, q * own_cells : (q + 1) * own_cells] = slab[p]

    def nominal(z, slot):
        level = 1.0 / z[species : species + 1]
        rate = jnp.exp(
            jnp.dot(
                w_nominal[...], stacked(z, -level, species, row), preferred_element_type=F32
            )
        )
        rates[slot] = rate
        high, low = halves(rate)
        production = jnp.dot(
            w_net[...], high.astype(BF16), preferred_element_type=F32
        ) + jnp.dot(w_net[...], low.astype(BF16), preferred_element_type=F32)
        inverse = jnp.exp(-z)
        inverse = jnp.concatenate([inverse[:base], jnp.where(row < species, inverse[base:], 1.0)], 0)
        inverses[slot] = inverse
        prods[slot] = jnp.concatenate(
            [production[:base], jnp.where(row < species, production[base:], 0.0)], 0
        )
        return with_heat(production, species, row) * inverse

    def tangent(u, z, slot, d):
        level = 1.0 / z[species : species + 1]
        change = jnp.dot(
            w_tangent[d],
            stacked(u, u[species : species + 1] * (level * level), species, row),
            preferred_element_type=F32,
        )
        moved = jnp.dot(
            w_net[...], (rates[slot] * change).astype(BF16), preferred_element_type=F32
        )
        return (with_heat(moved, species, row) - prods[slot] * u) * inverses[slot]

    def lap(low, x, high):
        return low + high + in_plane(x, lane) - 6.0 * x

    s_near_in.wait_recv()
    s_far.start()
    group_near = to_group(st.at[near_side, g], near_side, 2 + len(peers))
    for copy in group_near:
        copy.start()
    locals_[1].wait()
    arrived(1)
    for k in (1, 2):
        mid[k] = nominal(zs[k + 1], k)
    locals_[0].wait()
    span(0, cuts // 2, forward)
    s_far.wait_recv()
    group_far = to_group(st.at[far_side, g], far_side, 2 + 2 * len(peers))
    for copy in group_far:
        copy.start()
    span(cuts // 2, cuts, forward)

    def own_planes(d, carry):
        spread = spread_ref[...]
        unpack(1, d)
        for k in (1, 2):
            u = tt[k + 1, d]
            inner = tt[4 - k, d] + in_plane(u, lane) - 6.0 * u
            part[d, k - 1] = tangent(u, zs[k + 1], k, d) + spread * inner
        forward(cuts + d)
        return carry

    lax.fori_loop(0, directions, own_planes, 0)
    done = cuts + directions

    arrived(near_side)
    mid[near_k] = nominal(zs[near_k + 1], near_k)
    span(done, done + 1, forward)
    arrived(far_side)
    mid[far_k] = nominal(zs[far_k + 1], far_k)
    for k in range(4):
        z = zs[k + 1]
        rate = mid[k] + spread_ref[...] * lap(zs[k], z, zs[k + 2])
        mid[k] = z + TIME_STEP * rate
        if k in (1, 2):
            ns_full[k - 1] = z + 0.5 * TIME_STEP * rate
    span(done + 1, done + 2, forward)
    for k in (1, 2):
        z = mid[k]
        rate = nominal(z, k + 3) + spread_ref[...] * lap(mid[k - 1], z, mid[k + 1])
        ns_full[k - 1] += 0.5 * TIME_STEP * rate
    own = pl.ds(pl.multiple_of(g * own_cells, own_cells), own_cells)
    ns_ref[...] = jnp.swapaxes(ns_full[:, :, own], 0, 1)[:fields]
    span(done + 2, cuts * (directions - 1), forward)

    def halo(k, d):
        u = tt[k + 1, d]
        rate = tangent(u, zs[k + 1], k, d) + spread_ref[...] * lap(tt[k, d], u, tt[k + 2, d])
        mt[k] = u + TIME_STEP * rate

    def direction(d, carry):
        @pl.when(d == directions - 2)
        def _():
            span(cuts * (directions - 1), pieces, forward)

        unpack(near_side, d)
        halo(near_k, d)
        span(cuts * d, cuts * d + cuts, lambda c: far(c).wait_recv())
        unpack(far_side, d)
        spread = spread_ref[...]
        halo(far_k, d)
        for k in (1, 2):
            u = tt[k + 1, d]
            rate = part[d, k - 1] + spread * tt[3 * k - 2, d]
            mt[k] = u + TIME_STEP * rate
            part[d, k - 1] = u + 0.5 * TIME_STEP * rate
        for k in (1, 2):
            u = mt[k]
            rate = tangent(u, mid[k], k + 3, d) + spread * lap(mt[k - 1], u, mt[k + 1])
            part[d, k - 1] += 0.5 * TIME_STEP * rate
        lanes = t_ref.shape[3]
        tiles = [
            part[d, p, :, q * lanes : (q + 1) * lanes] for q in range(cells // lanes) for p in range(2)
        ]
        nt_ref[d] = jnp.swapaxes(jnp.stack(tiles, 0), 0, 1)[:fields]
        return carry

    lax.fori_loop(0, directions, direction, 0)

    s_near.wait_send()
    s_far.wait_send()
    for copy in group_own + group_near + group_far:
        copy.wait_send()

    def sent(c):
        near(c).wait_send()
        far(c).wait_send()

    span(0, pieces, sent)


def shards(
    flame_state, tangents, direction_index, reactant_table, product_table,
    natural_log_frequency, arrhenius_energy, diffusivity, enthalpy,
):
    fields, planes, own_cells = flame_state.shape
    directions, cells = tangents.shape[0], tangents.shape[3]
    reactions, species = reactant_table.shape
    groups, ring = lax.axis_size("grp"), lax.axis_size("sp")
    assert planes == 2 and ring % 2 == 0 and directions >= 3
    rows = -(-(species + 3) // 8) * 8
    assert species % 8 <= 5
    depth = -(-reactions // 16) * 16
    lanes = -(-reactions // 128) * 128
    tile = math.gcd(cells, 128)

    sens = tangents.reshape(directions, fields, planes, cells // tile, tile).transpose(0, 1, 3, 2, 4)
    sens = sens.reshape(directions, fields, planes * cells // tile, tile)

    vmem = pl.BlockSpec(memory_space=pltpu.VMEM)
    anywhere = pl.BlockSpec(memory_space=pl.ANY)
    hbm = pl.BlockSpec(memory_space=pltpu.HBM)
    pieces = math.gcd(fields, 9) * directions
    new_state, new_sens = pl.pallas_call(
        functools.partial(kernel, species, groups, ring),
        out_shape=(
            jax.ShapeDtypeStruct(flame_state.shape, F32),
            jax.ShapeDtypeStruct(sens.shape, F32),
        ),
        in_specs=[anywhere, anywhere] + [hbm] * 7,
        out_specs=(vmem, vmem),
        scratch_shapes=[
            pltpu.SMEM((directions,), jnp.int32),
            pltpu.VMEM((species, reactions), jnp.int32),
            pltpu.VMEM((species, reactions), jnp.int32),
            pltpu.VMEM((reactions,), F32),
            pltpu.VMEM((reactions,), F32),
            pltpu.VMEM((fields,), F32),
            pltpu.VMEM((species,), F32),
            pltpu.VMEM((depth, 2 * rows), BF16),
            pltpu.VMEM((directions, depth, 2 * rows), BF16),
            pltpu.VMEM((rows, depth), BF16),
            pltpu.VMEM((rows, cells), F32),
            pltpu.VMEM((2 * rows, lanes), F32),
            pltpu.VMEM((rows, lanes), F32),
            pltpu.VMEM((3,) + sens.shape, F32),
            pltpu.VMEM((3, groups) + flame_state.shape, F32),
            pltpu.VMEM((6, rows, cells), F32),
            pltpu.VMEM((4, rows, cells), F32),
            pltpu.VMEM((6, depth, cells), F32),
            pltpu.VMEM((6, rows, cells), F32),
            pltpu.VMEM((6, rows, cells), F32),
            pltpu.VMEM((6, directions, rows, cells), F32),
            pltpu.VMEM((4, rows, cells), F32),
            pltpu.VMEM((directions, 2, rows, cells), F32),
            pltpu.VMEM((2, rows, cells), F32),
            pltpu.SemaphoreType.DMA((2 + 3 * (groups - 1),)),
            pltpu.SemaphoreType.DMA((3, groups)),
            pltpu.SemaphoreType.DMA((pieces,)),
            pltpu.SemaphoreType.DMA((pieces,)),
            pltpu.SemaphoreType.DMA((pieces,)),
            pltpu.SemaphoreType.DMA((pieces,)),
            pltpu.SemaphoreType.DMA((9,)),
        ],
        compiler_params=pltpu.CompilerParams(
            collective_id=0, has_side_effects=True, vmem_limit_bytes=48 << 20
        ),
        name="step",
    )(
        *[
            pltpu.with_memory_space_constraint(x, pltpu.HBM)
            for x in (
                flame_state, sens, reactant_table.T, product_table.T, natural_log_frequency,
                arrhenius_energy, diffusivity, enthalpy, direction_index,
            )
        ],
    )
    new_sens = new_sens.reshape(directions, fields, cells // tile, planes, tile)
    return new_state, new_sens.transpose(0, 1, 3, 2, 4).reshape(tangents.shape)


def solution(mesh):
    in_specs = (
        P(None, "sp", "grp"), P("grp", None, "sp", None), P("grp"),
        P(), P(), P(), P(), P(), P(),
    )
    out_specs = (P(None, "sp", "grp"), P("grp", None, "sp", None))
    return jax.shard_map(shards, mesh=mesh, in_specs=in_specs, out_specs=out_specs, check_vma=False)
```
